256 devices in a mesh: depth: 8 (over y, x_lo), tile: 32 (over z, x_hi, core).
Axes of the slice: x: 4 (x_hi: 2, x_lo: 2; x = x_hi * 2 + x_lo), y: 4, z: 8, core: 2. Of those that a mesh axis runs over, the one named last changes fastest.
Arguments:
- warm_field: float32 [16, 2, 16, 256, 256], P(None, None, 'depth', 'tile'), may hold values from -6 to 6
- slowness_sq: float32 [16, 256, 256], P('depth', 'tile'), may hold values from 1.2 to 2.6
- adjoint_field: float32 [16, 2, 16, 256, 256], P(None, None, 'depth', 'tile'), may hold values from -6 to 6
- observed: float32 [16, 2, 256], replicated, may hold values from -6 to 6
- source_cell: int32 [16], replicated, may hold values from 0 to 1048575
- receiver_cell: int32 [16, 256], replicated, may hold values from 0 to 1048575
- pml_width: int32 [4], replicated, may hold values from 2 to 4
Outputs:
- new_field: float32 [16, 2, 16, 256, 256], P(None, None, 'depth', 'tile')
- misfit: float32 [16], replicated
- gradient: float32 [16, 256, 256], P('depth', 'tile')
The draws below stay inside these ranges and needn't reach their ends.
All inputs are finite; a program needn't handle non-finite values.
Results may differ from the reference program's by a relative error of at most 0.00002.
Values sent between devices are 32-bit elements; how exact they have to be, the bound alone decides.
A program may use at most 64 MiB of HBM per device.

```python
import jax
import jax.numpy as jnp

SHOTS = 16
NY = 256
RECS = 256
NZ = 16
NX = 256


def draw_warm_field(key, part):
    depth_rise = jnp.arange(NZ, dtype=jnp.float32) / (NZ - 1.0)
    width_rise = jnp.arange(NX, dtype=jnp.float32) / (NX - 1.0)
    envelope = 0.5 + depth_rise[:, None] + 0.5 * width_rise[None, :]
    shape_full = (SHOTS, 2, NZ, NX, NY)
    values_raw = jax.random.truncated_normal(key, -3.0, 3.0, shape_full, jnp.float32)
    return (values_raw * envelope[None, None, :, :, None]).astype(jnp.float32)


def draw_slowness_sq(key, part):
    shape_full = (NZ, NX, NY)
    seeded = jax.random.fold_in(key, 7)
    low_log = jnp.log(jnp.float32(1.2))
    high_log = jnp.log(jnp.float32(2.6))
    values_raw = jnp.exp(jax.random.uniform(seeded, shape_full, jnp.float32, low_log, high_log))
    values_raw = jnp.clip(values_raw, 1.2, 2.6)
    return values_raw.astype(jnp.float32)


def with_ends(entries, rng, least, high):
    dims = entries.shape
    place = [jax.random.randint(jax.random.fold_in(rng, axis), (), 0, dims[axis]) for axis in range(len(dims))]
    entries = entries.at[tuple(place)].set(least)
    longest = dims.index(max(dims))
    place[longest] = (place[longest] + 1) % dims[longest]
    return entries.at[tuple(place)].set(high)


def levels(own_key, dims, split, low, largest):
    def one(position, parts):
        steps = jax.random.uniform(jax.random.fold_in(jax.random.fold_in(own_key, 6), position), (parts,), jnp.float32, low / len(split), largest / len(split))
        return jnp.repeat(jnp.exp(steps), dims[position] // parts).reshape((-1,) + (1,) * (len(dims) - position - 1))

    loudness = one(*split[0])
    for cut in split[1:]:
        loudness = loudness * one(*cut)
    return loudness


def noise(own_key, shape, scale, bound, cuts=(), kind=jnp.bfloat16):
    array = scale * jax.random.normal(own_key, shape, jnp.float32)
    if cuts:
        array = array * levels(own_key, shape, cuts, -0.22, 0.18)
    return jnp.clip(array, -bound, bound).astype(kind)


def setup_inputs(seed: int = 0) -> dict:
    streams_of = jax.random.split(jax.random.key(seed), 8)
    warm_field = draw_warm_field(jax.random.fold_in(streams_of[7], 71), 0)
    slowness_sq = draw_slowness_sq(jax.random.fold_in(streams_of[7], 71), 0)
    adjoint_field = noise(streams_of[2], (SHOTS, 2, NZ, NX, NY), 1.0, 6.0, ((2, 8), (3, 32)), jnp.float32)
    observed = noise(streams_of[3], (SHOTS, 2, RECS), 1.0, 6.0, (), jnp.float32)
    source_cell = with_ends(jax.random.randint(streams_of[4], (SHOTS,), 0, NZ * NX * NY), jax.random.fold_in(streams_of[4], 1), 0, (NZ * NX * NY) - 1).astype(jnp.int32)
    receiver_cell = with_ends(jax.random.randint(streams_of[5], (SHOTS, RECS), 0, NZ * NX * NY), jax.random.fold_in(streams_of[5], 1), 0, (NZ * NX * NY) - 1).astype(jnp.int32)
    pml_width = with_ends(jax.random.randint(streams_of[6], (4,), 2, 5), jax.random.fold_in(streams_of[6], 1), 2, 4).astype(jnp.int32)
    return {"warm_field": warm_field, "slowness_sq": slowness_sq, "adjoint_field": adjoint_field, "observed": observed, "source_cell": source_cell, "receiver_cell": receiver_cell, "pml_width": pml_width}


WAVE_SCALE = 1.9
PML_DAMP = 2.0
SOURCE_AMPLITUDE = 25.0
SHIFT_IMAG = 0.5
CENTER_WEIGHT = 128.0 / 30.0
LUMPED_DIAG = 2.0
LAP_WEIGHTS = (0.0, 14.0 / 30.0, 3.0 / 30.0, 1.0 / 30.0)
MASS_WEIGHTS = (1.0 / 6.0, 2.0 / 3.0, 1.0 / 6.0)


def damping_ramp(distance, extent):
    fraction = jnp.maximum((extent - distance) / extent, 0.0)
    return fraction * fraction


def damping_field(pml_width, depth_pos, width_pos, full_depth, full_width):
    widths = pml_width.astype(jnp.float32)
    depth_part = damping_ramp(depth_pos, widths[0]) + damping_ramp(full_depth - 1.0 - depth_pos, widths[1])
    width_part = damping_ramp(width_pos, widths[2]) + damping_ramp(full_width - 1.0 - width_pos, widths[3])
    return PML_DAMP * (depth_part[:, None] + width_part[None, :])


def pad_last_two(values):
    return jnp.pad(values, [(0, 0)] * (values.ndim - 2) + [(1, 1), (1, 1)])


def laplacian_from_padded(padded, depth_len, width_len, long_len):
    summed = CENTER_WEIGHT * padded[..., 1:1 + depth_len, 1:1 + width_len, 1:1 + long_len]
    for off_depth in (-1, 0, 1):
        for off_width in (-1, 0, 1):
            for off_long in (-1, 0, 1):
                order_no = abs(off_depth) + abs(off_width) + abs(off_long)
                if order_no > 0:
                    summed = summed - LAP_WEIGHTS[order_no] * padded[..., 1 + off_depth:1 + off_depth + depth_len, 1 + off_width:1 + off_width + width_len, 1 + off_long:1 + off_long + long_len]
    return summed


def lateral_smooth(padded, width_len, long_len):
    summed = None
    for off_width in range(3):
        for off_long in range(3):
            weighted = MASS_WEIGHTS[off_width] * MASS_WEIGHTS[off_long] * padded[..., off_width:off_width + width_len, off_long:off_long + long_len]
            summed = weighted if summed is None else summed + weighted
    return summed


def plane_coupling(padded, width_len, long_len):
    summed = None
    for off_width in range(3):
        for off_long in range(3):
            order_no = 1 + (off_width != 1) + (off_long != 1)
            weighted = LAP_WEIGHTS[order_no] * padded[..., off_width:off_width + width_len, off_long:off_long + long_len]
            summed = weighted if summed is None else summed + weighted
    return summed


def combine_operator(negative, mass, damping):
    real_out = negative[:, 0] - WAVE_SCALE * (mass[:, 0] - damping * mass[:, 1])
    imag_out = negative[:, 1] - WAVE_SCALE * (mass[:, 1] + damping * mass[:, 0])
    return jnp.stack([real_out, imag_out], axis=1)


def inverse_diagonal(slowness, damping):
    scaled = WAVE_SCALE * MASS_WEIGHTS[1] * MASS_WEIGHTS[1] * slowness
    diag_re = LUMPED_DIAG - scaled * (1.0 + SHIFT_IMAG * damping)
    diag_im = -scaled * (damping + SHIFT_IMAG)
    norm_sq = diag_re * diag_re + diag_im * diag_im
    return diag_re / norm_sq, -diag_im / norm_sq


def complex_scale(inv_re, inv_im, values):
    real_part = values[:, 0]
    imag_part = values[:, 1]
    return jnp.stack([inv_re * real_part - inv_im * imag_part, inv_re * imag_part + inv_im * real_part], axis=1)


def apply_operator(values, slowness, damping):
    depth_len, width_len, long_len = slowness.shape
    padded = jnp.pad(values, [(0, 0), (0, 0), (1, 1), (1, 1), (1, 1)])
    negative = laplacian_from_padded(padded, depth_len, width_len, long_len)
    mass = lateral_smooth(pad_last_two(values * slowness), width_len, long_len)
    return combine_operator(negative, mass, damping)


def couple(plane_in):
    return plane_coupling(pad_last_two(plane_in), plane_in.shape[-2], plane_in.shape[-1])


def precondition(residual, inv_re, inv_im):
    previous = jnp.zeros_like(residual[:, :, 0])
    downward = []
    for layer_no in range(NZ):
        source_term = residual[:, :, layer_no] + couple(previous)
        previous = complex_scale(inv_re[layer_no], inv_im[layer_no], source_term)
        downward.append(previous)
    upward = [None] * NZ
    previous = jnp.zeros_like(residual[:, :, 0])
    for layer_no in range(NZ - 1, -1, -1):
        previous = downward[layer_no] + complex_scale(inv_re[layer_no], inv_im[layer_no], couple(previous))
        upward[layer_no] = previous
    return jnp.stack(upward, axis=2)


def reference(warm_field, slowness_sq, adjoint_field, observed, source_cell, receiver_cell, pml_width):
    depth_pos = jnp.arange(NZ).astype(jnp.float32)
    width_pos = jnp.arange(NX).astype(jnp.float32)
    damping = damping_field(pml_width, depth_pos, width_pos, NZ * 1.0, NX * 1.0)[:, :, None]
    cells = jnp.arange(NZ * NX * NY, dtype=jnp.int32).reshape(NZ, NX, NY)
    hits = cells[None] == source_cell[:, None, None, None]
    source_re = jnp.where(hits, SOURCE_AMPLITUDE, 0.0).astype(warm_field.dtype)
    forcing = jnp.stack([source_re, jnp.zeros_like(source_re)], axis=1)
    residual = forcing - apply_operator(warm_field, slowness_sq, damping)
    inv_re, inv_im = inverse_diagonal(slowness_sq, damping)
    search = precondition(residual, inv_re, inv_im)
    image_field = apply_operator(search, slowness_sq, damping)
    dot_real = jnp.sum(image_field[:, 0] * residual[:, 0] + image_field[:, 1] * residual[:, 1], axis=(1, 2, 3))
    dot_imag = jnp.sum(image_field[:, 0] * residual[:, 1] - image_field[:, 1] * residual[:, 0], axis=(1, 2, 3))
    image_norm = jnp.sum(image_field[:, 0] * image_field[:, 0] + image_field[:, 1] * image_field[:, 1], axis=(1, 2, 3))
    step_re = (dot_real / image_norm)[:, None, None, None]
    step_im = (dot_imag / image_norm)[:, None, None, None]
    new_re = warm_field[:, 0] + step_re * search[:, 0] - step_im * search[:, 1]
    new_im = warm_field[:, 1] + step_re * search[:, 1] + step_im * search[:, 0]
    new_field = jnp.stack([new_re, new_im], axis=1)
    flattened = new_field.reshape(SHOTS, 2, NZ * NX * NY)
    sampled = jnp.take_along_axis(flattened, jnp.broadcast_to(receiver_cell[:, None, :], (SHOTS, 2, RECS)), axis=2)
    data_miss = sampled - observed
    misfit = 0.5 * jnp.sum(data_miss * data_miss, axis=(1, 2))
    adjoint_re = adjoint_field[:, 0]
    adjoint_im = adjoint_field[:, 1]
    weight_re = adjoint_re + damping * adjoint_im
    weight_im = damping * adjoint_re - adjoint_im
    smooth_re = lateral_smooth(pad_last_two(weight_re), NX, NY)
    smooth_im = lateral_smooth(pad_last_two(weight_im), NX, NY)
    gradient = (-WAVE_SCALE / SHOTS) * jnp.sum(new_re * smooth_re - new_im * smooth_im, axis=0)
    return (new_field, misfit, gradient)
```

```python
import jax
import jax.numpy as jnp
from jax import lax
from jax.sharding import PartitionSpec as P

WAVE_SCALE = 1.9
PML_DAMP = 2.0
SOURCE_AMPLITUDE = 25.0
SHIFT_IMAG = 0.5
CENTER_WEIGHT = 128.0 / 30.0
LUMPED_DIAG = 2.0
LAP_WEIGHTS = (0.0, 14.0 / 30.0, 3.0 / 30.0, 1.0 / 30.0)
MASS_WEIGHTS = (1.0 / 6.0, 2.0 / 3.0, 1.0 / 6.0)


def extended(shard, sides, width):
    for axis, dim in sides:
        size, length = (lax.axis_size(axis), shard.shape[dim])
        up = [(i, (i + 1) % size) for i in range(size - 1)]
        down = [(j, i) for i, j in up]
        last = lax.slice_in_dim(shard, length - width, length, axis=dim)
        leading = lax.slice_in_dim(shard, 0, width, axis=dim)
        before = lax.ppermute(last, axis, up)
        after = lax.ppermute(leading, axis, down)
        shard = jnp.concatenate([before, shard, after], axis=dim)
    return shard


def shifted(value, axis, steps):
    count = lax.axis_size(axis)
    leading, last = (max(0, -steps), min(count, count - steps))
    return lax.ppermute(value, axis, [(source, source + steps) for source in range(leading, last)])


def damping_ramp(distance, extent):
    fraction = jnp.maximum((extent - distance) / extent, 0.0)
    return fraction * fraction


def damping_field(pml_width, depth_pos, width_pos, full_depth, full_width):
    widths = pml_width.astype(jnp.float32)
    depth_part = damping_ramp(depth_pos, widths[0]) + damping_ramp(
        full_depth - 1.0 - depth_pos, widths[1]
    )
    width_part = damping_ramp(width_pos, widths[2]) + damping_ramp(
        full_width - 1.0 - width_pos, widths[3]
    )
    return PML_DAMP * (depth_part[:, None] + width_part[None, :])


def pad_long(values):
    return jnp.pad(values, [(0, 0)] * (values.ndim - 1) + [(1, 1)])


def laplacian_from_padded(padded, depth_len, width_len, long_len):
    summed = CENTER_WEIGHT * padded[..., 1 : 1 + depth_len, 1 : 1 + width_len, 1 : 1 + long_len]
    for off_depth in (-1, 0, 1):
        for off_width in (-1, 0, 1):
            for off_long in (-1, 0, 1):
                order_no = abs(off_depth) + abs(off_width) + abs(off_long)
                if order_no > 0:
                    summed = (
                        summed
                        - LAP_WEIGHTS[order_no]
                        * padded[
                            ...,
                            1 + off_depth : 1 + off_depth + depth_len,
                            1 + off_width : 1 + off_width + width_len,
                            1 + off_long : 1 + off_long + long_len,
                        ]
                    )
    return summed


def lateral_smooth(padded, width_len, long_len):
    summed = None
    for off_width in range(3):
        for off_long in range(3):
            weighted = (
                MASS_WEIGHTS[off_width]
                * MASS_WEIGHTS[off_long]
                * padded[..., off_width : off_width + width_len, off_long : off_long + long_len]
            )
            summed = weighted if summed is None else summed + weighted
    return summed


def plane_coupling(padded, width_len, long_len):
    summed = None
    for off_width in range(3):
        for off_long in range(3):
            order_no = 1 + (off_width != 1) + (off_long != 1)
            weighted = (
                LAP_WEIGHTS[order_no]
                * padded[..., off_width : off_width + width_len, off_long : off_long + long_len]
            )
            summed = weighted if summed is None else summed + weighted
    return summed


def combine_operator(negative, mass, damping):
    real_out = negative[:, 0] - WAVE_SCALE * (mass[:, 0] - damping * mass[:, 1])
    imag_out = negative[:, 1] - WAVE_SCALE * (mass[:, 1] + damping * mass[:, 0])
    return jnp.stack([real_out, imag_out], axis=1)


def inverse_diagonal(slowness, damping):
    scaled = WAVE_SCALE * MASS_WEIGHTS[1] * MASS_WEIGHTS[1] * slowness
    diag_re = LUMPED_DIAG - scaled * (1.0 + SHIFT_IMAG * damping)
    diag_im = -scaled * (damping + SHIFT_IMAG)
    norm_sq = diag_re * diag_re + diag_im * diag_im
    return (diag_re / norm_sq, -diag_im / norm_sq)


def complex_scale(inv_re, inv_im, values):
    real_part = values[:, 0]
    imag_part = values[:, 1]
    return jnp.stack(
        [inv_re * real_part - inv_im * imag_part, inv_re * imag_part + inv_im * real_part], axis=1
    )


def per_device(
    warm_field, slowness_sq, adjoint_field, observed, source_cell, receiver_cell, pml_width
):
    shot_count, _, layer_len, width_len, long_len = warm_field.shape
    depth_index = lax.axis_index("depth")
    tile_index = lax.axis_index("tile")
    depth_count = lax.axis_size("depth")
    tile_count = lax.axis_size("tile")
    full_depth = layer_len * depth_count
    full_width = width_len * tile_count
    depth_cells = depth_index * layer_len + jnp.arange(layer_len, dtype=jnp.int32)
    width_cells = tile_index * width_len + jnp.arange(width_len, dtype=jnp.int32)
    width_wide = (tile_index * width_len - 1 + jnp.arange(width_len + 2, dtype=jnp.int32)).astype(
        jnp.float32
    )
    damping_wide = damping_field(
        pml_width, depth_cells.astype(jnp.float32), width_wide, full_depth * 1.0, full_width * 1.0
    )[:, :, None]
    damping = damping_wide[:, 1:-1]
    slowness_wide = extended(slowness_sq, (("tile", 1),), 1)

    def apply_operator(values):
        padded = extended(values, (("depth", 2), ("tile", 3)), 1)
        negative = laplacian_from_padded(pad_long(padded), layer_len, width_len, long_len)
        mass = lateral_smooth(pad_long(padded[:, :, 1:-1] * slowness_wide), width_len, long_len)
        return combine_operator(negative, mass, damping)

    cell_index = (
        depth_cells[:, None, None] * full_width + width_cells[None, :, None]
    ) * long_len + jnp.arange(long_len, dtype=jnp.int32)[None, None, :]
    hits = cell_index[None] == source_cell[:, None, None, None]
    source_re = jnp.where(hits, SOURCE_AMPLITUDE, 0.0).astype(jnp.float32)
    forcing = jnp.stack([source_re, jnp.zeros_like(source_re)], axis=1)
    residual = forcing - apply_operator(warm_field)
    inv_re, inv_im = inverse_diagonal(slowness_sq, damping)

    def couple(plane_in):
        with_rims = extended(plane_in, (("tile", 2),), 1)
        return plane_coupling(pad_long(with_rims), width_len, long_len)

    def down_section(source_part, incoming):
        previous = incoming
        layers_out = []
        for layer_no in range(layer_len):
            source_term = source_part[:, :, layer_no] + couple(previous)
            previous = complex_scale(inv_re[layer_no], inv_im[layer_no], source_term)
            layers_out.append(previous)
        return jnp.stack(layers_out, axis=2)

    def up_section(downward_part, incoming):
        previous = incoming
        layers_out = [None] * layer_len
        for layer_no in range(layer_len - 1, -1, -1):
            previous = downward_part[:, :, layer_no] + complex_scale(
                inv_re[layer_no], inv_im[layer_no], couple(previous)
            )
            layers_out[layer_no] = previous
        return jnp.stack(layers_out, axis=2)

    groups = 1
    per_group = shot_count // groups

    def run_chain(inputs, downward):
        position = depth_index if downward else depth_count - 1 - depth_index

        def segment_body(segment_no, state_pair):
            result, outgoing = state_pair
            if downward:
                incoming = shifted(outgoing, "depth", 1)
            else:
                incoming = shifted(outgoing, "depth", -1)
            group_no = segment_no - position
            is_valid = jnp.logical_and(group_no >= 0, group_no < groups)
            group_start = jnp.clip(group_no, 0, groups - 1) * per_group
            if downward:
                updated = down_section(inputs, incoming)
                edge_plane = updated[:, :, layer_len - 1]
            else:
                updated = up_section(inputs, incoming)
                edge_plane = updated[:, :, 0]
            current = result
            result = lax.dynamic_update_slice_in_dim(
                result, jnp.where(is_valid, updated, current), group_start, 0
            )
            outgoing = jnp.where(is_valid, edge_plane, outgoing)
            return (result, outgoing)

        initial = (
            jnp.zeros_like(inputs),
            jnp.zeros((per_group, 2, width_len, long_len), jnp.float32),
        )
        final_pair = lax.fori_loop(0, depth_count + groups - 1, segment_body, initial)
        return final_pair[0]

    downward = run_chain(residual, True)
    search = run_chain(downward, False)
    image_field = apply_operator(search)
    local_real = jnp.sum(
        image_field[:, 0] * residual[:, 0] + image_field[:, 1] * residual[:, 1], axis=(1, 2, 3)
    )
    local_imag = jnp.sum(
        image_field[:, 0] * residual[:, 1] - image_field[:, 1] * residual[:, 0], axis=(1, 2, 3)
    )
    local_norm = jnp.sum(
        image_field[:, 0] * image_field[:, 0] + image_field[:, 1] * image_field[:, 1],
        axis=(1, 2, 3),
    )
    plane_cells = full_width * long_len
    rec_depth = receiver_cell // plane_cells
    rec_width = receiver_cell // long_len % full_width
    rec_long = receiver_cell % long_len
    local_depth = rec_depth - depth_index * layer_len
    local_width = rec_width - tile_index * width_len
    is_owned = (
        (local_depth >= 0)
        & (local_depth < layer_len)
        & (local_width >= 0)
        & (local_width < width_len)
    )
    row_count = layer_len * width_len
    local_row = jnp.where(is_owned, local_depth * width_len + local_width, -1)
    row_hot = (local_row[:, :, None] == jnp.arange(row_count, dtype=jnp.int32)).astype(jnp.float32)
    both_fields = jnp.concatenate([warm_field, search], axis=1).reshape(
        shot_count, 4, row_count, long_len
    )
    picked_rows = jnp.einsum(
        "srk,sqky->sqry", row_hot, both_fields, precision=lax.Precision.HIGHEST
    )
    col_hot = rec_long[:, None, :, None] == jnp.arange(long_len, dtype=jnp.int32)
    picked = jnp.sum(jnp.where(col_hot, picked_rows, 0.0), axis=-1)
    packed = jnp.concatenate(
        [jnp.stack([local_real, local_imag, local_norm], axis=1), picked.reshape(shot_count, -1)],
        axis=1,
    )
    packed = lax.psum(packed, ("depth", "tile"))
    dot_real, dot_imag, image_norm = packed[:, 0], packed[:, 1], packed[:, 2]
    picked = packed[:, 3:].reshape(shot_count, 4, -1)
    step_re = (dot_real / image_norm)[:, None, None, None]
    step_im = (dot_imag / image_norm)[:, None, None, None]
    new_re = warm_field[:, 0] + step_re * search[:, 0] - step_im * search[:, 1]
    new_im = warm_field[:, 1] + step_re * search[:, 1] + step_im * search[:, 0]
    new_field = jnp.stack([new_re, new_im], axis=1)
    rec_re = (dot_real / image_norm)[:, None]
    rec_im = (dot_imag / image_norm)[:, None]
    sampled_re = picked[:, 0] + rec_re * picked[:, 2] - rec_im * picked[:, 3]
    sampled_im = picked[:, 1] + rec_re * picked[:, 3] + rec_im * picked[:, 2]
    miss_re = sampled_re - observed[:, 0]
    miss_im = sampled_im - observed[:, 1]
    misfit = 0.5 * jnp.sum(miss_re * miss_re + miss_im * miss_im, axis=1)
    adjoint_wide = extended(adjoint_field, (("tile", 3),), 1)
    adjoint_re = adjoint_wide[:, 0]
    adjoint_im = adjoint_wide[:, 1]
    weight_re = adjoint_re + damping_wide * adjoint_im
    weight_im = damping_wide * adjoint_re - adjoint_im
    smooth_re = lateral_smooth(pad_long(weight_re), width_len, long_len)
    smooth_im = lateral_smooth(pad_long(weight_im), width_len, long_len)
    gradient = -WAVE_SCALE / shot_count * jnp.sum(new_re * smooth_re - new_im * smooth_im, axis=0)
    return (new_field, misfit, gradient)


def solution(mesh):
    return jax.shard_map(
        per_device,
        mesh=mesh,
        in_specs=(
            P(None, None, "depth", "tile", None),
            P("depth", "tile", None),
            P(None, None, "depth", "tile", None),
            P(),
            P(),
            P(),
            P(),
        ),
        out_specs=(P(None, None, "depth", "tile", None), P(), P("depth", "tile", None)),
        check_vma=False,
    )
```

```python
import jax
import jax.numpy as jnp
from jax import lax
from jax.sharding import PartitionSpec as P

WAVE_SCALE = 1.9
PML_DAMP = 2.0
SOURCE_AMPLITUDE = 25.0
SHIFT_IMAG = 0.5
CENTER_WEIGHT = 128.0 / 30.0
LUMPED_DIAG = 2.0
LAP_WEIGHTS = (0.0, 14.0 / 30.0, 3.0 / 30.0, 1.0 / 30.0)
MASS_WEIGHTS = (1.0 / 6.0, 2.0 / 3.0, 1.0 / 6.0)


def extended(shard, sides, width):
    for axis, dim in sides:
        size, length = (lax.axis_size(axis), shard.shape[dim])
        up = [(i, (i + 1) % size) for i in range(size - 1)]
        down = [(j, i) for i, j in up]
        last = lax.slice_in_dim(shard, length - width, length, axis=dim)
        leading = lax.slice_in_dim(shard, 0, width, axis=dim)
        before = lax.ppermute(last, axis, up)
        after = lax.ppermute(leading, axis, down)
        shard = jnp.concatenate([before, shard, after], axis=dim)
    return shard


def shifted(value, axis, steps):
    count = lax.axis_size(axis)
    leading, last = (max(0, -steps), min(count, count - steps))
    return lax.ppermute(value, axis, [(source, source + steps) for source in range(leading, last)])


def damping_ramp(distance, extent):
    fraction = jnp.maximum((extent - distance) / extent, 0.0)
    return fraction * fraction


def damping_field(pml_width, depth_pos, width_pos, full_depth, full_width):
    widths = pml_width.astype(jnp.float32)
    depth_part = damping_ramp(depth_pos, widths[0]) + damping_ramp(
        full_depth - 1.0 - depth_pos, widths[1]
    )
    width_part = damping_ramp(width_pos, widths[2]) + damping_ramp(
        full_width - 1.0 - width_pos, widths[3]
    )
    return PML_DAMP * (depth_part[:, None] + width_part[None, :])


def pad_long(values):
    return jnp.pad(values, [(0, 0)] * (values.ndim - 1) + [(1, 1)])


def laplacian_from_padded(padded, depth_len, width_len, long_len):
    summed = CENTER_WEIGHT * padded[..., 1 : 1 + depth_len, 1 : 1 + width_len, 1 : 1 + long_len]
    for off_depth in (-1, 0, 1):
        for off_width in (-1, 0, 1):
            for off_long in (-1, 0, 1):
                order_no = abs(off_depth) + abs(off_width) + abs(off_long)
                if order_no > 0:
                    summed = (
                        summed
                        - LAP_WEIGHTS[order_no]
                        * padded[
                            ...,
                            1 + off_depth : 1 + off_depth + depth_len,
                            1 + off_width : 1 + off_width + width_len,
                            1 + off_long : 1 + off_long + long_len,
                        ]
                    )
    return summed


def lateral_smooth(padded, width_len, long_len):
    summed = None
    for off_width in range(3):
        for off_long in range(3):
            weighted = (
                MASS_WEIGHTS[off_width]
                * MASS_WEIGHTS[off_long]
                * padded[..., off_width : off_width + width_len, off_long : off_long + long_len]
            )
            summed = weighted if summed is None else summed + weighted
    return summed


def plane_coupling(padded, width_len, long_len):
    summed = None
    for off_width in range(3):
        for off_long in range(3):
            order_no = 1 + (off_width != 1) + (off_long != 1)
            weighted = (
                LAP_WEIGHTS[order_no]
                * padded[..., off_width : off_width + width_len, off_long : off_long + long_len]
            )
            summed = weighted if summed is None else summed + weighted
    return summed


def combine_operator(negative, mass, damping):
    real_out = negative[:, 0] - WAVE_SCALE * (mass[:, 0] - damping * mass[:, 1])
    imag_out = negative[:, 1] - WAVE_SCALE * (mass[:, 1] + damping * mass[:, 0])
    return jnp.stack([real_out, imag_out], axis=1)


def inverse_diagonal(slowness, damping):
    scaled = WAVE_SCALE * MASS_WEIGHTS[1] * MASS_WEIGHTS[1] * slowness
    diag_re = LUMPED_DIAG - scaled * (1.0 + SHIFT_IMAG * damping)
    diag_im = -scaled * (damping + SHIFT_IMAG)
    norm_sq = diag_re * diag_re + diag_im * diag_im
    return (diag_re / norm_sq, -diag_im / norm_sq)


def complex_scale(inv_re, inv_im, values):
    real_part = values[:, 0]
    imag_part = values[:, 1]
    return jnp.stack(
        [inv_re * real_part - inv_im * imag_part, inv_re * imag_part + inv_im * real_part], axis=1
    )


def per_device(
    warm_field, slowness_sq, adjoint_field, observed, source_cell, receiver_cell, pml_width
):
    shot_count, _, layer_len, width_len, long_len = warm_field.shape
    depth_index = lax.axis_index("depth")
    tile_index = lax.axis_index("tile")
    depth_count = lax.axis_size("depth")
    tile_count = lax.axis_size("tile")
    full_depth = layer_len * depth_count
    full_width = width_len * tile_count
    depth_cells = depth_index * layer_len + jnp.arange(layer_len, dtype=jnp.int32)
    width_cells = tile_index * width_len + jnp.arange(width_len, dtype=jnp.int32)
    width_wide = (tile_index * width_len - 1 + jnp.arange(width_len + 2, dtype=jnp.int32)).astype(
        jnp.float32
    )
    damping_wide = damping_field(
        pml_width, depth_cells.astype(jnp.float32), width_wide, full_depth * 1.0, full_width * 1.0
    )[:, :, None]
    damping = damping_wide[:, 1:-1]
    slowness_wide = extended(slowness_sq, (("tile", 1),), 1)

    def apply_operator(values):
        padded = extended(values, (("depth", 2), ("tile", 3)), 1)
        negative = laplacian_from_padded(pad_long(padded), layer_len, width_len, long_len)
        mass = lateral_smooth(pad_long(padded[:, :, 1:-1] * slowness_wide), width_len, long_len)
        return combine_operator(negative, mass, damping)

    cell_index = (
        depth_cells[:, None, None] * full_width + width_cells[None, :, None]
    ) * long_len + jnp.arange(long_len, dtype=jnp.int32)[None, None, :]
    hits = cell_index[None] == source_cell[:, None, None, None]
    source_re = jnp.where(hits, SOURCE_AMPLITUDE, 0.0).astype(jnp.float32)
    forcing = jnp.stack([source_re, jnp.zeros_like(source_re)], axis=1)
    residual = forcing - apply_operator(warm_field)

    shots_here = shot_count // depth_count
    reach = -(-(full_depth - 1) // width_len)
    halo = reach * width_len
    window = width_len + 2 * halo

    def with_neighbour_rows(block):
        pieces = [shifted(block, "tile", step) for step in range(reach, 0, -1)]
        pieces.append(block)
        pieces += [shifted(block, "tile", -step) for step in range(1, reach + 1)]
        return jnp.concatenate(pieces, axis=-2)

    spread = jnp.broadcast_to(slowness_sq[None], (depth_count,) + slowness_sq.shape)
    slowness_all = lax.all_to_all(spread, "depth", 0, 1, tiled=True)[0]
    slowness_ext = with_neighbour_rows(slowness_all)
    rows_ext = tile_index * width_len - halo + jnp.arange(window, dtype=jnp.int32)
    damping_ext = damping_field(
        pml_width,
        jnp.arange(full_depth, dtype=jnp.float32),
        rows_ext.astype(jnp.float32),
        full_depth * 1.0,
        full_width * 1.0,
    )[:, :, None]
    inv_re, inv_im = inverse_diagonal(slowness_ext, damping_ext)
    row_valid = ((rows_ext >= 0) & (rows_ext < full_width))[:, None]

    def couple(plane_in):
        return plane_coupling(
            jnp.pad(plane_in, [(0, 0)] * (plane_in.ndim - 2) + [(1, 1), (1, 1)]),
            window,
            long_len,
        )

    residual_t = lax.all_to_all(residual, "depth", 0, 2, tiled=True)
    residual_ext = with_neighbour_rows(residual_t)
    previous = jnp.zeros((shots_here, 2, window, long_len), jnp.float32)
    layers_out = []
    for layer_no in range(full_depth):
        source_term = residual_ext[:, :, layer_no] + couple(previous)
        previous = jnp.where(
            row_valid, complex_scale(inv_re[layer_no], inv_im[layer_no], source_term), 0.0
        )
        layers_out.append(previous[:, :, halo : halo + width_len])
    downward_t = jnp.stack(layers_out, axis=2)
    downward_ext = with_neighbour_rows(downward_t)
    previous = jnp.zeros((shots_here, 2, window, long_len), jnp.float32)
    layers_out = [None] * full_depth
    for layer_no in range(full_depth - 1, -1, -1):
        previous = jnp.where(
            row_valid,
            downward_ext[:, :, layer_no]
            + complex_scale(inv_re[layer_no], inv_im[layer_no], couple(previous)),
            0.0,
        )
        layers_out[layer_no] = previous[:, :, halo : halo + width_len]
    search_t = jnp.stack(layers_out, axis=2)
    search = lax.all_to_all(search_t, "depth", 2, 0, tiled=True)
    image_field = apply_operator(search)
    local_real = jnp.sum(
        image_field[:, 0] * residual[:, 0] + image_field[:, 1] * residual[:, 1], axis=(1, 2, 3)
    )
    local_imag = jnp.sum(
        image_field[:, 0] * residual[:, 1] - image_field[:, 1] * residual[:, 0], axis=(1, 2, 3)
    )
    local_norm = jnp.sum(
        image_field[:, 0] * image_field[:, 0] + image_field[:, 1] * image_field[:, 1],
        axis=(1, 2, 3),
    )
    dot_real, dot_imag, image_norm = lax.psum(
        (local_real, local_imag, local_norm), ("depth", "tile")
    )
    step_re = (dot_real / image_norm)[:, None, None, None]
    step_im = (dot_imag / image_norm)[:, None, None, None]
    new_re = warm_field[:, 0] + step_re * search[:, 0] - step_im * search[:, 1]
    new_im = warm_field[:, 1] + step_re * search[:, 1] + step_im * search[:, 0]
    new_field = jnp.stack([new_re, new_im], axis=1)
    plane_cells = full_width * long_len
    rec_depth = receiver_cell // plane_cells
    rec_width = receiver_cell // long_len % full_width
    rec_long = receiver_cell % long_len
    local_depth = rec_depth - depth_index * layer_len
    local_width = rec_width - tile_index * width_len
    is_owned = (
        (local_depth >= 0)
        & (local_depth < layer_len)
        & (local_width >= 0)
        & (local_width < width_len)
    )
    row_count = layer_len * width_len
    local_row = jnp.where(is_owned, local_depth * width_len + local_width, -1)
    row_hot = (local_row[:, :, None] == jnp.arange(row_count, dtype=jnp.int32)).astype(jnp.float32)
    picked_rows = jnp.einsum(
        "srk,sqky->sqry",
        row_hot,
        new_field.reshape(shot_count, 2, row_count, long_len),
        precision=lax.Precision.HIGHEST,
    )
    col_hot = rec_long[:, None, :, None] == jnp.arange(long_len, dtype=jnp.int32)
    sampled = jnp.sum(jnp.where(col_hot, picked_rows, 0.0), axis=-1)
    data_miss = sampled - observed
    squared = jnp.sum(data_miss * data_miss, axis=1)
    partial_misfit = 0.5 * jnp.sum(jnp.where(is_owned, squared, 0.0), axis=1)
    misfit = lax.psum(partial_misfit, ("depth", "tile"))
    adjoint_wide = extended(adjoint_field, (("tile", 3),), 1)
    adjoint_re = adjoint_wide[:, 0]
    adjoint_im = adjoint_wide[:, 1]
    weight_re = adjoint_re + damping_wide * adjoint_im
    weight_im = damping_wide * adjoint_re - adjoint_im
    smooth_re = lateral_smooth(pad_long(weight_re), width_len, long_len)
    smooth_im = lateral_smooth(pad_long(weight_im), width_len, long_len)
    gradient = -WAVE_SCALE / shot_count * jnp.sum(new_re * smooth_re - new_im * smooth_im, axis=0)
    return (new_field, misfit, gradient)


def solution(mesh):
    return jax.shard_map(
        per_device,
        mesh=mesh,
        in_specs=(
            P(None, None, "depth", "tile", None),
            P("depth", "tile", None),
            P(None, None, "depth", "tile", None),
            P(),
            P(),
            P(),
            P(),
        ),
        out_specs=(P(None, None, "depth", "tile", None), P(), P("depth", "tile", None)),
        check_vma=False,
    )
```

```python
import jax
import jax.numpy as jnp
from jax import lax
from jax.sharding import PartitionSpec as P

WAVE_SCALE = 1.9
PML_DAMP = 2.0
SOURCE_AMPLITUDE = 25.0
SHIFT_IMAG = 0.5
CENTER_WEIGHT = 128.0 / 30.0
LUMPED_DIAG = 2.0
LAP_WEIGHTS = (0.0, 14.0 / 30.0, 3.0 / 30.0, 1.0 / 30.0)
MASS_WEIGHTS = (1.0 / 6.0, 2.0 / 3.0, 1.0 / 6.0)


def extended(shard, sides, width):
    for axis, dim in sides:
        size, length = (lax.axis_size(axis), shard.shape[dim])
        up = [(i, (i + 1) % size) for i in range(size - 1)]
        down = [(j, i) for i, j in up]
        last = lax.slice_in_dim(shard, length - width, length, axis=dim)
        leading = lax.slice_in_dim(shard, 0, width, axis=dim)
        before = lax.ppermute(last, axis, up)
        after = lax.ppermute(leading, axis, down)
        shard = jnp.concatenate([before, shard, after], axis=dim)
    return shard


def shifted(value, axis, steps):
    count = lax.axis_size(axis)
    leading, last = (max(0, -steps), min(count, count - steps))
    return lax.ppermute(value, axis, [(source, source + steps) for source in range(leading, last)])


def damping_ramp(distance, extent):
    fraction = jnp.maximum((extent - distance) / extent, 0.0)
    return fraction * fraction


def damping_field(pml_width, depth_pos, width_pos, full_depth, full_width):
    widths = pml_width.astype(jnp.float32)
    depth_part = damping_ramp(depth_pos, widths[0]) + damping_ramp(
        full_depth - 1.0 - depth_pos, widths[1]
    )
    width_part = damping_ramp(width_pos, widths[2]) + damping_ramp(
        full_width - 1.0 - width_pos, widths[3]
    )
    return PML_DAMP * (depth_part[:, None] + width_part[None, :])


def pad_long(values):
    return jnp.pad(values, [(0, 0)] * (values.ndim - 1) + [(1, 1)])


def laplacian_from_padded(padded, depth_len, width_len, long_len):
    summed = CENTER_WEIGHT * padded[..., 1 : 1 + depth_len, 1 : 1 + width_len, 1 : 1 + long_len]
    for off_depth in (-1, 0, 1):
        for off_width in (-1, 0, 1):
            for off_long in (-1, 0, 1):
                order_no = abs(off_depth) + abs(off_width) + abs(off_long)
                if order_no > 0:
                    summed = (
                        summed
                        - LAP_WEIGHTS[order_no]
                        * padded[
                            ...,
                            1 + off_depth : 1 + off_depth + depth_len,
                            1 + off_width : 1 + off_width + width_len,
                            1 + off_long : 1 + off_long + long_len,
                        ]
                    )
    return summed


def lateral_smooth(padded, width_len, long_len):
    summed = None
    for off_width in range(3):
        for off_long in range(3):
            weighted = (
                MASS_WEIGHTS[off_width]
                * MASS_WEIGHTS[off_long]
                * padded[..., off_width : off_width + width_len, off_long : off_long + long_len]
            )
            summed = weighted if summed is None else summed + weighted
    return summed


def plane_coupling(padded, width_len, long_len):
    summed = None
    for off_width in range(3):
        for off_long in range(3):
            order_no = 1 + (off_width != 1) + (off_long != 1)
            weighted = (
                LAP_WEIGHTS[order_no]
                * padded[..., off_width : off_width + width_len, off_long : off_long + long_len]
            )
            summed = weighted if summed is None else summed + weighted
    return summed


def combine_operator(negative, mass, damping):
    real_out = negative[:, 0] - WAVE_SCALE * (mass[:, 0] - damping * mass[:, 1])
    imag_out = negative[:, 1] - WAVE_SCALE * (mass[:, 1] + damping * mass[:, 0])
    return jnp.stack([real_out, imag_out], axis=1)


def inverse_diagonal(slowness, damping):
    scaled = WAVE_SCALE * MASS_WEIGHTS[1] * MASS_WEIGHTS[1] * slowness
    diag_re = LUMPED_DIAG - scaled * (1.0 + SHIFT_IMAG * damping)
    diag_im = -scaled * (damping + SHIFT_IMAG)
    norm_sq = diag_re * diag_re + diag_im * diag_im
    return (diag_re / norm_sq, -diag_im / norm_sq)


def complex_scale(inv_re, inv_im, values):
    real_part = values[:, 0]
    imag_part = values[:, 1]
    return jnp.stack(
        [inv_re * real_part - inv_im * imag_part, inv_re * imag_part + inv_im * real_part], axis=1
    )


def per_device(
    warm_field, slowness_sq, adjoint_field, observed, source_cell, receiver_cell, pml_width
):
    shot_count, _, layer_len, width_len, long_len = warm_field.shape
    depth_index = lax.axis_index("depth")
    tile_index = lax.axis_index("tile")
    depth_count = lax.axis_size("depth")
    tile_count = lax.axis_size("tile")
    full_depth = layer_len * depth_count
    full_width = width_len * tile_count
    depth_cells = depth_index * layer_len + jnp.arange(layer_len, dtype=jnp.int32)
    width_cells = tile_index * width_len + jnp.arange(width_len, dtype=jnp.int32)
    width_wide = (tile_index * width_len - 1 + jnp.arange(width_len + 2, dtype=jnp.int32)).astype(
        jnp.float32
    )
    damping_wide = damping_field(
        pml_width, depth_cells.astype(jnp.float32), width_wide, full_depth * 1.0, full_width * 1.0
    )[:, :, None]
    damping = damping_wide[:, 1:-1]
    slowness_wide = extended(slowness_sq, (("tile", 1),), 1)

    def apply_operator(values):
        padded = extended(values, (("depth", 2), ("tile", 3)), 1)
        negative = laplacian_from_padded(pad_long(padded), layer_len, width_len, long_len)
        mass = lateral_smooth(pad_long(padded[:, :, 1:-1] * slowness_wide), width_len, long_len)
        return combine_operator(negative, mass, damping)

    cell_index = (
        depth_cells[:, None, None] * full_width + width_cells[None, :, None]
    ) * long_len + jnp.arange(long_len, dtype=jnp.int32)[None, None, :]
    hits = cell_index[None] == source_cell[:, None, None, None]
    source_re = jnp.where(hits, SOURCE_AMPLITUDE, 0.0).astype(jnp.float32)
    forcing = jnp.stack([source_re, jnp.zeros_like(source_re)], axis=1)
    residual = forcing - apply_operator(warm_field)

    shots_here = shot_count // depth_count
    reach = -(-(full_depth - 1) // width_len)
    halo = reach * width_len
    window = width_len + 2 * halo

    def with_neighbour_rows(block):
        pieces = [shifted(block, "tile", step) for step in range(reach, 0, -1)]
        pieces.append(block)
        pieces += [shifted(block, "tile", -step) for step in range(1, reach + 1)]
        return jnp.concatenate(pieces, axis=-2)

    spread = jnp.broadcast_to(slowness_sq[None], (depth_count,) + slowness_sq.shape)
    slowness_all = lax.all_to_all(spread, "depth", 0, 1, tiled=True)[0]
    slowness_ext = with_neighbour_rows(slowness_all)
    rows_ext = tile_index * width_len - halo + jnp.arange(window, dtype=jnp.int32)
    damping_ext = damping_field(
        pml_width,
        jnp.arange(full_depth, dtype=jnp.float32),
        rows_ext.astype(jnp.float32),
        full_depth * 1.0,
        full_width * 1.0,
    )[:, :, None]
    inv_re, inv_im = inverse_diagonal(slowness_ext, damping_ext)
    row_valid = ((rows_ext >= 0) & (rows_ext < full_width))[:, None]

    def couple(plane_in):
        return plane_coupling(
            jnp.pad(plane_in, [(0, 0)] * (plane_in.ndim - 2) + [(1, 1), (1, 1)]),
            window,
            long_len,
        )

    residual_t = lax.all_to_all(residual, "depth", 0, 2, tiled=True)
    residual_ext = with_neighbour_rows(residual_t)
    previous = jnp.zeros((shots_here, 2, window, long_len), jnp.float32)
    layers_out = []
    for layer_no in range(full_depth):
        source_term = residual_ext[:, :, layer_no] + couple(previous)
        previous = jnp.where(
            row_valid, complex_scale(inv_re[layer_no], inv_im[layer_no], source_term), 0.0
        )
        layers_out.append(previous[:, :, halo : halo + width_len])
    downward_t = jnp.stack(layers_out, axis=2)
    downward_ext = with_neighbour_rows(downward_t)
    previous = jnp.zeros((shots_here, 2, window, long_len), jnp.float32)
    layers_out = [None] * full_depth
    for layer_no in range(full_depth - 1, -1, -1):
        previous = jnp.where(
            row_valid,
            downward_ext[:, :, layer_no]
            + complex_scale(inv_re[layer_no], inv_im[layer_no], couple(previous)),
            0.0,
        )
        layers_out[layer_no] = previous[:, :, halo : halo + width_len]
    search_t = jnp.stack(layers_out, axis=2)
    search = lax.all_to_all(search_t, "depth", 2, 0, tiled=True)
    image_field = apply_operator(search)
    local_real = jnp.sum(
        image_field[:, 0] * residual[:, 0] + image_field[:, 1] * residual[:, 1], axis=(1, 2, 3)
    )
    local_imag = jnp.sum(
        image_field[:, 0] * residual[:, 1] - image_field[:, 1] * residual[:, 0], axis=(1, 2, 3)
    )
    local_norm = jnp.sum(
        image_field[:, 0] * image_field[:, 0] + image_field[:, 1] * image_field[:, 1],
        axis=(1, 2, 3),
    )
    plane_cells = full_width * long_len
    rec_depth = receiver_cell // plane_cells
    rec_width = receiver_cell // long_len % full_width
    rec_long = receiver_cell % long_len
    local_depth = rec_depth - depth_index * layer_len
    local_width = rec_width - tile_index * width_len
    is_owned = (
        (local_depth >= 0)
        & (local_depth < layer_len)
        & (local_width >= 0)
        & (local_width < width_len)
    )
    row_count = layer_len * width_len
    local_row = jnp.where(is_owned, local_depth * width_len + local_width, -1)
    row_hot = (local_row[:, :, None] == jnp.arange(row_count, dtype=jnp.int32)).astype(jnp.float32)
    both_fields = jnp.concatenate([warm_field, search], axis=1).reshape(
        shot_count, 4, row_count, long_len
    )
    picked_rows = jnp.einsum(
        "srk,sqky->sqry", row_hot, both_fields, precision=lax.Precision.HIGHEST
    )
    col_hot = rec_long[:, None, :, None] == jnp.arange(long_len, dtype=jnp.int32)
    picked = jnp.sum(jnp.where(col_hot, picked_rows, 0.0), axis=-1)
    gap_re = picked[:, 0] - observed[:, 0]
    gap_im = picked[:, 1] - observed[:, 1]
    dir_re = picked[:, 2]
    dir_im = picked[:, 3]

    def owned_sum(values):
        return jnp.sum(jnp.where(is_owned, values, 0.0), axis=1)

    gap_norm = owned_sum(gap_re * gap_re + gap_im * gap_im)
    cross_re = owned_sum(gap_re * dir_re + gap_im * dir_im)
    cross_im = owned_sum(gap_re * dir_im - gap_im * dir_re)
    dir_norm = owned_sum(dir_re * dir_re + dir_im * dir_im)
    packed = jnp.stack(
        [local_real, local_imag, local_norm, gap_norm, cross_re, cross_im, dir_norm], axis=1
    )
    packed = lax.psum(packed, ("depth", "tile"))
    dot_real, dot_imag, image_norm = packed[:, 0], packed[:, 1], packed[:, 2]
    gap_norm, cross_re, cross_im, dir_norm = packed[:, 3], packed[:, 4], packed[:, 5], packed[:, 6]
    step_re = (dot_real / image_norm)[:, None, None, None]
    step_im = (dot_imag / image_norm)[:, None, None, None]
    new_re = warm_field[:, 0] + step_re * search[:, 0] - step_im * search[:, 1]
    new_im = warm_field[:, 1] + step_re * search[:, 1] + step_im * search[:, 0]
    new_field = jnp.stack([new_re, new_im], axis=1)
    scale_re = dot_real / image_norm
    scale_im = dot_imag / image_norm
    misfit = 0.5 * (
        gap_norm
        + 2.0 * (scale_re * cross_re - scale_im * cross_im)
        + (scale_re * scale_re + scale_im * scale_im) * dir_norm
    )
    adjoint_wide = extended(adjoint_field, (("tile", 3),), 1)
    adjoint_re = adjoint_wide[:, 0]
    adjoint_im = adjoint_wide[:, 1]
    weight_re = adjoint_re + damping_wide * adjoint_im
    weight_im = damping_wide * adjoint_re - adjoint_im
    smooth_re = lateral_smooth(pad_long(weight_re), width_len, long_len)
    smooth_im = lateral_smooth(pad_long(weight_im), width_len, long_len)
    gradient = -WAVE_SCALE / shot_count * jnp.sum(new_re * smooth_re - new_im * smooth_im, axis=0)
    return (new_field, misfit, gradient)


def solution(mesh):
    return jax.shard_map(
        per_device,
        mesh=mesh,
        in_specs=(
            P(None, None, "depth", "tile", None),
            P("depth", "tile", None),
            P(None, None, "depth", "tile", None),
            P(),
            P(),
            P(),
            P(),
        ),
        out_specs=(P(None, None, "depth", "tile", None), P(), P("depth", "tile", None)),
        check_vma=False,
    )
```

```python
import jax
import jax.numpy as jnp
from jax import lax
from jax.sharding import PartitionSpec as P
from jax.experimental import pallas as pl
from jax.experimental.pallas import tpu as pltpu
import functools

WAVE_SCALE = 1.9
PML_DAMP = 2.0
SOURCE_AMPLITUDE = 25.0
SHIFT_IMAG = 0.5
CENTER_WEIGHT = 128.0 / 30.0
LUMPED_DIAG = 2.0
LAP_WEIGHTS = (0.0, 14.0 / 30.0, 3.0 / 30.0, 1.0 / 30.0)
MASS_WEIGHTS = (1.0 / 6.0, 2.0 / 3.0, 1.0 / 6.0)


def extended(shard, sides, width):
    for axis, dim in sides:
        size, length = (lax.axis_size(axis), shard.shape[dim])
        up = [(i, (i + 1) % size) for i in range(size - 1)]
        down = [(j, i) for i, j in up]
        last = lax.slice_in_dim(shard, length - width, length, axis=dim)
        leading = lax.slice_in_dim(shard, 0, width, axis=dim)
        before = lax.ppermute(last, axis, up)
        after = lax.ppermute(leading, axis, down)
        shard = jnp.concatenate([before, shard, after], axis=dim)
    return shard


def shifted(value, axis, steps):
    count = lax.axis_size(axis)
    leading, last = (max(0, -steps), min(count, count - steps))
    return lax.ppermute(value, axis, [(source, source + steps) for source in range(leading, last)])


def all_sum_kernel(depth_count, tile_count, x_ref, out_ref, tile_slots, depth_slots, part,
                   copy_sem, tile_send, tile_recv, depth_send, depth_recv):
    me_d = lax.axis_index("depth")
    me_t = lax.axis_index("tile")
    mesh_ids = pl.DeviceIdType.MESH
    barrier = pltpu.get_barrier_semaphore()
    for k in range(1, tile_count):
        pl.semaphore_signal(barrier, inc=1, device_id=(me_d, lax.rem(me_t + k, tile_count)),
                            device_id_type=mesh_ids)
    for k in range(1, depth_count):
        pl.semaphore_signal(barrier, inc=1, device_id=(lax.rem(me_d + k, depth_count), me_t),
                            device_id_type=mesh_ids)
    pl.semaphore_wait(barrier, tile_count + depth_count - 2)

    def exchange(src, slots, send_sems, recv_sems, me, count, peer_of):
        own = pltpu.make_async_copy(src, slots.at[me], copy_sem)
        own.start()
        sends = []
        for k in range(1, count):
            copy = pltpu.make_async_remote_copy(
                src_ref=src, dst_ref=slots.at[me], send_sem=send_sems.at[k],
                recv_sem=recv_sems.at[me], device_id=peer_of(lax.rem(me + k, count)),
                device_id_type=mesh_ids)
            copy.start()
            sends.append(copy)
        own.wait()
        for k in range(1, count):
            sender = lax.rem(me + count - k, count)
            pltpu.make_async_remote_copy(
                src_ref=src, dst_ref=slots.at[sender], send_sem=send_sems.at[k],
                recv_sem=recv_sems.at[sender], device_id=peer_of(sender),
                device_id_type=mesh_ids).wait_recv()
        for copy in sends:
            copy.wait_send()
        total = slots[0]
        for j in range(1, count):
            total = total + slots[j]
        return total

    part[...] = exchange(x_ref, tile_slots, tile_send, tile_recv, me_t, tile_count,
                         lambda t: (me_d, t))
    out_ref[...] = exchange(part, depth_slots, depth_send, depth_recv, me_d, depth_count,
                            lambda d: (d, me_t))


def all_sum(values):
    depth_count = lax.axis_size("depth")
    tile_count = lax.axis_size("tile")
    size = values.size
    block = 8 * 128
    padded = -(-size // block) * block
    flat = jnp.pad(values.reshape(-1), (0, padded - size)).reshape(padded // 128, 128)
    summed = pl.pallas_call(
        functools.partial(all_sum_kernel, depth_count, tile_count),
        out_shape=jax.ShapeDtypeStruct(flat.shape, jnp.float32),
        in_specs=[pl.BlockSpec(memory_space=pltpu.VMEM)],
        out_specs=pl.BlockSpec(memory_space=pltpu.VMEM),
        scratch_shapes=[
            pltpu.VMEM((tile_count,) + flat.shape, jnp.float32),
            pltpu.VMEM((depth_count,) + flat.shape, jnp.float32),
            pltpu.VMEM(flat.shape, jnp.float32),
            pltpu.SemaphoreType.DMA,
            pltpu.SemaphoreType.DMA((tile_count,)),
            pltpu.SemaphoreType.DMA((tile_count,)),
            pltpu.SemaphoreType.DMA((depth_count,)),
            pltpu.SemaphoreType.DMA((depth_count,)),
        ],
        compiler_params=pltpu.CompilerParams(collective_id=0, has_side_effects=True),
    )(flat)
    return summed.reshape(-1)[:size].reshape(values.shape)


def damping_ramp(distance, extent):
    fraction = jnp.maximum((extent - distance) / extent, 0.0)
    return fraction * fraction


def damping_field(pml_width, depth_pos, width_pos, full_depth, full_width):
    widths = pml_width.astype(jnp.float32)
    depth_part = damping_ramp(depth_pos, widths[0]) + damping_ramp(
        full_depth - 1.0 - depth_pos, widths[1]
    )
    width_part = damping_ramp(width_pos, widths[2]) + damping_ramp(
        full_width - 1.0 - width_pos, widths[3]
    )
    return PML_DAMP * (depth_part[:, None] + width_part[None, :])


def pad_long(values):
    return jnp.pad(values, [(0, 0)] * (values.ndim - 1) + [(1, 1)])


def laplacian_from_padded(padded, depth_len, width_len, long_len):
    summed = CENTER_WEIGHT * padded[..., 1 : 1 + depth_len, 1 : 1 + width_len, 1 : 1 + long_len]
    for off_depth in (-1, 0, 1):
        for off_width in (-1, 0, 1):
            for off_long in (-1, 0, 1):
                order_no = abs(off_depth) + abs(off_width) + abs(off_long)
                if order_no > 0:
                    summed = (
                        summed
                        - LAP_WEIGHTS[order_no]
                        * padded[
                            ...,
                            1 + off_depth : 1 + off_depth + depth_len,
                            1 + off_width : 1 + off_width + width_len,
                            1 + off_long : 1 + off_long + long_len,
                        ]
                    )
    return summed


def lateral_smooth(padded, width_len, long_len):
    summed = None
    for off_width in range(3):
        for off_long in range(3):
            weighted = (
                MASS_WEIGHTS[off_width]
                * MASS_WEIGHTS[off_long]
                * padded[..., off_width : off_width + width_len, off_long : off_long + long_len]
            )
            summed = weighted if summed is None else summed + weighted
    return summed


def plane_coupling(padded, width_len, long_len):
    summed = None
    for off_width in range(3):
        for off_long in range(3):
            order_no = 1 + (off_width != 1) + (off_long != 1)
            weighted = (
                LAP_WEIGHTS[order_no]
                * padded[..., off_width : off_width + width_len, off_long : off_long + long_len]
            )
            summed = weighted if summed is None else summed + weighted
    return summed


def combine_operator(negative, mass, damping):
    real_out = negative[:, 0] - WAVE_SCALE * (mass[:, 0] - damping * mass[:, 1])
    imag_out = negative[:, 1] - WAVE_SCALE * (mass[:, 1] + damping * mass[:, 0])
    return jnp.stack([real_out, imag_out], axis=1)


def inverse_diagonal(slowness, damping):
    scaled = WAVE_SCALE * MASS_WEIGHTS[1] * MASS_WEIGHTS[1] * slowness
    diag_re = LUMPED_DIAG - scaled * (1.0 + SHIFT_IMAG * damping)
    diag_im = -scaled * (damping + SHIFT_IMAG)
    norm_sq = diag_re * diag_re + diag_im * diag_im
    return (diag_re / norm_sq, -diag_im / norm_sq)


def complex_scale(inv_re, inv_im, values):
    real_part = values[:, 0]
    imag_part = values[:, 1]
    return jnp.stack(
        [inv_re * real_part - inv_im * imag_part, inv_re * imag_part + inv_im * real_part], axis=1
    )


def per_device(
    warm_field, slowness_sq, adjoint_field, observed, source_cell, receiver_cell, pml_width
):
    shot_count, _, layer_len, width_len, long_len = warm_field.shape
    depth_index = lax.axis_index("depth")
    tile_index = lax.axis_index("tile")
    depth_count = lax.axis_size("depth")
    tile_count = lax.axis_size("tile")
    full_depth = layer_len * depth_count
    full_width = width_len * tile_count
    depth_cells = depth_index * layer_len + jnp.arange(layer_len, dtype=jnp.int32)
    width_cells = tile_index * width_len + jnp.arange(width_len, dtype=jnp.int32)
    width_wide = (tile_index * width_len - 1 + jnp.arange(width_len + 2, dtype=jnp.int32)).astype(
        jnp.float32
    )
    damping_wide = damping_field(
        pml_width, depth_cells.astype(jnp.float32), width_wide, full_depth * 1.0, full_width * 1.0
    )[:, :, None]
    damping = damping_wide[:, 1:-1]
    slowness_wide = extended(slowness_sq, (("tile", 1),), 1)

    def apply_operator(values):
        padded = extended(values, (("depth", 2), ("tile", 3)), 1)
        negative = laplacian_from_padded(pad_long(padded), layer_len, width_len, long_len)
        mass = lateral_smooth(pad_long(padded[:, :, 1:-1] * slowness_wide), width_len, long_len)
        return combine_operator(negative, mass, damping)

    cell_index = (
        depth_cells[:, None, None] * full_width + width_cells[None, :, None]
    ) * long_len + jnp.arange(long_len, dtype=jnp.int32)[None, None, :]
    hits = cell_index[None] == source_cell[:, None, None, None]
    source_re = jnp.where(hits, SOURCE_AMPLITUDE, 0.0).astype(jnp.float32)
    forcing = jnp.stack([source_re, jnp.zeros_like(source_re)], axis=1)
    residual = forcing - apply_operator(warm_field)

    shots_here = shot_count // depth_count
    reach = -(-(full_depth - 1) // width_len)
    halo = reach * width_len
    window = width_len + 2 * halo

    def with_neighbour_rows(block):
        pieces = [shifted(block, "tile", step) for step in range(reach, 0, -1)]
        pieces.append(block)
        pieces += [shifted(block, "tile", -step) for step in range(1, reach + 1)]
        return jnp.concatenate(pieces, axis=-2)

    spread = jnp.broadcast_to(slowness_sq[None], (depth_count,) + slowness_sq.shape)
    slowness_all = lax.all_to_all(spread, "depth", 0, 1, tiled=True)[0]
    slowness_ext = with_neighbour_rows(slowness_all)
    rows_ext = tile_index * width_len - halo + jnp.arange(window, dtype=jnp.int32)
    damping_ext = damping_field(
        pml_width,
        jnp.arange(full_depth, dtype=jnp.float32),
        rows_ext.astype(jnp.float32),
        full_depth * 1.0,
        full_width * 1.0,
    )[:, :, None]
    inv_re, inv_im = inverse_diagonal(slowness_ext, damping_ext)
    row_valid = ((rows_ext >= 0) & (rows_ext < full_width))[:, None]

    def couple(plane_in):
        return plane_coupling(
            jnp.pad(plane_in, [(0, 0)] * (plane_in.ndim - 2) + [(1, 1), (1, 1)]),
            window,
            long_len,
        )

    residual_t = lax.all_to_all(residual, "depth", 0, 2, tiled=True)
    residual_ext = with_neighbour_rows(residual_t)
    previous = jnp.zeros((shots_here, 2, window, long_len), jnp.float32)
    layers_out = []
    for layer_no in range(full_depth):
        source_term = residual_ext[:, :, layer_no] + couple(previous)
        previous = jnp.where(
            row_valid, complex_scale(inv_re[layer_no], inv_im[layer_no], source_term), 0.0
        )
        layers_out.append(previous[:, :, halo : halo + width_len])
    downward_t = jnp.stack(layers_out, axis=2)
    downward_ext = with_neighbour_rows(downward_t)
    previous = jnp.zeros((shots_here, 2, window, long_len), jnp.float32)
    layers_out = [None] * full_depth
    for layer_no in range(full_depth - 1, -1, -1):
        previous = jnp.where(
            row_valid,
            downward_ext[:, :, layer_no]
            + complex_scale(inv_re[layer_no], inv_im[layer_no], couple(previous)),
            0.0,
        )
        layers_out[layer_no] = previous[:, :, halo : halo + width_len]
    search_t = jnp.stack(layers_out, axis=2)
    search = lax.all_to_all(search_t, "depth", 2, 0, tiled=True)
    image_field = apply_operator(search)
    local_real = jnp.sum(
        image_field[:, 0] * residual[:, 0] + image_field[:, 1] * residual[:, 1], axis=(1, 2, 3)
    )
    local_imag = jnp.sum(
        image_field[:, 0] * residual[:, 1] - image_field[:, 1] * residual[:, 0], axis=(1, 2, 3)
    )
    local_norm = jnp.sum(
        image_field[:, 0] * image_field[:, 0] + image_field[:, 1] * image_field[:, 1],
        axis=(1, 2, 3),
    )
    plane_cells = full_width * long_len
    rec_depth = receiver_cell // plane_cells
    rec_width = receiver_cell // long_len % full_width
    rec_long = receiver_cell % long_len
    local_depth = rec_depth - depth_index * layer_len
    local_width = rec_width - tile_index * width_len
    is_owned = (
        (local_depth >= 0)
        & (local_depth < layer_len)
        & (local_width >= 0)
        & (local_width < width_len)
    )
    row_count = layer_len * width_len
    local_row = jnp.where(is_owned, local_depth * width_len + local_width, -1)
    row_hot = (local_row[:, :, None] == jnp.arange(row_count, dtype=jnp.int32)).astype(jnp.float32)
    both_fields = jnp.concatenate([warm_field, search], axis=1).reshape(
        shot_count, 4, row_count, long_len
    )
    picked_rows = jnp.einsum(
        "srk,sqky->sqry", row_hot, both_fields, precision=lax.Precision.HIGHEST
    )
    col_hot = rec_long[:, None, :, None] == jnp.arange(long_len, dtype=jnp.int32)
    picked = jnp.sum(jnp.where(col_hot, picked_rows, 0.0), axis=-1)
    gap_re = picked[:, 0] - observed[:, 0]
    gap_im = picked[:, 1] - observed[:, 1]
    dir_re = picked[:, 2]
    dir_im = picked[:, 3]

    def owned_sum(values):
        return jnp.sum(jnp.where(is_owned, values, 0.0), axis=1)

    gap_norm = owned_sum(gap_re * gap_re + gap_im * gap_im)
    cross_re = owned_sum(gap_re * dir_re + gap_im * dir_im)
    cross_im = owned_sum(gap_re * dir_im - gap_im * dir_re)
    dir_norm = owned_sum(dir_re * dir_re + dir_im * dir_im)
    packed = jnp.stack(
        [local_real, local_imag, local_norm, gap_norm, cross_re, cross_im, dir_norm], axis=1
    )
    packed = all_sum(packed)
    dot_real, dot_imag, image_norm = packed[:, 0], packed[:, 1], packed[:, 2]
    gap_norm, cross_re, cross_im, dir_norm = packed[:, 3], packed[:, 4], packed[:, 5], packed[:, 6]
    step_re = (dot_real / image_norm)[:, None, None, None]
    step_im = (dot_imag / image_norm)[:, None, None, None]
    new_re = warm_field[:, 0] + step_re * search[:, 0] - step_im * search[:, 1]
    new_im = warm_field[:, 1] + step_re * search[:, 1] + step_im * search[:, 0]
    new_field = jnp.stack([new_re, new_im], axis=1)
    scale_re = dot_real / image_norm
    scale_im = dot_imag / image_norm
    misfit = 0.5 * (
        gap_norm
        + 2.0 * (scale_re * cross_re - scale_im * cross_im)
        + (scale_re * scale_re + scale_im * scale_im) * dir_norm
    )
    adjoint_wide = extended(adjoint_field, (("tile", 3),), 1)
    adjoint_re = adjoint_wide[:, 0]
    adjoint_im = adjoint_wide[:, 1]
    weight_re = adjoint_re + damping_wide * adjoint_im
    weight_im = damping_wide * adjoint_re - adjoint_im
    smooth_re = lateral_smooth(pad_long(weight_re), width_len, long_len)
    smooth_im = lateral_smooth(pad_long(weight_im), width_len, long_len)
    gradient = -WAVE_SCALE / shot_count * jnp.sum(new_re * smooth_re - new_im * smooth_im, axis=0)
    return (new_field, misfit, gradient)


def solution(mesh):
    return jax.shard_map(
        per_device,
        mesh=mesh,
        in_specs=(
            P(None, None, "depth", "tile", None),
            P("depth", "tile", None),
            P(None, None, "depth", "tile", None),
            P(),
            P(),
            P(),
            P(),
        ),
        out_specs=(P(None, None, "depth", "tile", None), P(), P("depth", "tile", None)),
        check_vma=False,
    )
```

```python
import jax
import jax.numpy as jnp
from jax import lax
from jax.sharding import PartitionSpec as P
from jax.experimental import pallas as pl
from jax.experimental.pallas import tpu as pltpu
import functools

WAVE_SCALE = 1.9
PML_DAMP = 2.0
SOURCE_AMPLITUDE = 25.0
SHIFT_IMAG = 0.5
CENTER_WEIGHT = 128.0 / 30.0
LUMPED_DIAG = 2.0
LAP_WEIGHTS = (0.0, 14.0 / 30.0, 3.0 / 30.0, 1.0 / 30.0)
MASS_WEIGHTS = (1.0 / 6.0, 2.0 / 3.0, 1.0 / 6.0)


def extended(shard, sides, width):
    for axis, dim in sides:
        size, length = (lax.axis_size(axis), shard.shape[dim])
        up = [(i, (i + 1) % size) for i in range(size - 1)]
        down = [(j, i) for i, j in up]
        last = lax.slice_in_dim(shard, length - width, length, axis=dim)
        leading = lax.slice_in_dim(shard, 0, width, axis=dim)
        before = lax.ppermute(last, axis, up)
        after = lax.ppermute(leading, axis, down)
        shard = jnp.concatenate([before, shard, after], axis=dim)
    return shard


def shifted(value, axis, steps):
    count = lax.axis_size(axis)
    leading, last = (max(0, -steps), min(count, count - steps))
    return lax.ppermute(value, axis, [(source, source + steps) for source in range(leading, last)])


def all_sum_kernel(depth_count, tile_count, x_ref, out_ref, tile_slots, depth_slots, part,
                   copy_sem, tile_send, tile_recv, depth_send, depth_recv):
    me_d = lax.axis_index("depth")
    me_t = lax.axis_index("tile")
    mesh_ids = pl.DeviceIdType.MESH
    barrier = pltpu.get_barrier_semaphore()
    for k in range(1, tile_count):
        pl.semaphore_signal(barrier, inc=1, device_id=(me_d, lax.rem(me_t + k, tile_count)),
                            device_id_type=mesh_ids)
    for k in range(1, depth_count):
        pl.semaphore_signal(barrier, inc=1, device_id=(lax.rem(me_d + k, depth_count), me_t),
                            device_id_type=mesh_ids)
    pl.semaphore_wait(barrier, tile_count + depth_count - 2)

    def exchange(src, slots, send_sems, recv_sems, me, count, peer_of):
        own = pltpu.make_async_copy(src, slots.at[me], copy_sem)
        own.start()
        sends = []
        for k in range(1, count):
            copy = pltpu.make_async_remote_copy(
                src_ref=src, dst_ref=slots.at[me], send_sem=send_sems.at[k],
                recv_sem=recv_sems.at[me], device_id=peer_of(lax.rem(me + k, count)),
                device_id_type=mesh_ids)
            copy.start()
            sends.append(copy)
        own.wait()
        for k in range(1, count):
            sender = lax.rem(me + count - k, count)
            pltpu.make_async_remote_copy(
                src_ref=src, dst_ref=slots.at[sender], send_sem=send_sems.at[k],
                recv_sem=recv_sems.at[sender], device_id=peer_of(sender),
                device_id_type=mesh_ids).wait_recv()
        for copy in sends:
            copy.wait_send()
        total = slots[0]
        for j in range(1, count):
            total = total + slots[j]
        return total

    part[...] = exchange(x_ref, tile_slots, tile_send, tile_recv, me_t, tile_count,
                         lambda t: (me_d, t))
    out_ref[...] = exchange(part, depth_slots, depth_send, depth_recv, me_d, depth_count,
                            lambda d: (d, me_t))


def all_sum(values):
    depth_count = lax.axis_size("depth")
    tile_count = lax.axis_size("tile")
    size = values.size
    block = 8 * 128
    padded = -(-size // block) * block
    flat = jnp.pad(values.reshape(-1), (0, padded - size)).reshape(padded // 128, 128)
    summed = pl.pallas_call(
        functools.partial(all_sum_kernel, depth_count, tile_count),
        out_shape=jax.ShapeDtypeStruct(flat.shape, jnp.float32),
        in_specs=[pl.BlockSpec(memory_space=pltpu.VMEM)],
        out_specs=pl.BlockSpec(memory_space=pltpu.VMEM),
        scratch_shapes=[
            pltpu.VMEM((tile_count,) + flat.shape, jnp.float32),
            pltpu.VMEM((depth_count,) + flat.shape, jnp.float32),
            pltpu.VMEM(flat.shape, jnp.float32),
            pltpu.SemaphoreType.DMA,
            pltpu.SemaphoreType.DMA((tile_count,)),
            pltpu.SemaphoreType.DMA((tile_count,)),
            pltpu.SemaphoreType.DMA((depth_count,)),
            pltpu.SemaphoreType.DMA((depth_count,)),
        ],
        compiler_params=pltpu.CompilerParams(collective_id=0, has_side_effects=True),
    )(flat)
    return summed.reshape(-1)[:size].reshape(values.shape)


def damping_ramp(distance, extent):
    fraction = jnp.maximum((extent - distance) / extent, 0.0)
    return fraction * fraction


def damping_field(pml_width, depth_pos, width_pos, full_depth, full_width):
    widths = pml_width.astype(jnp.float32)
    depth_part = damping_ramp(depth_pos, widths[0]) + damping_ramp(
        full_depth - 1.0 - depth_pos, widths[1]
    )
    width_part = damping_ramp(width_pos, widths[2]) + damping_ramp(
        full_width - 1.0 - width_pos, widths[3]
    )
    return PML_DAMP * (depth_part[:, None] + width_part[None, :])


def pad_long(values):
    return jnp.pad(values, [(0, 0)] * (values.ndim - 1) + [(1, 1)])


def laplacian_from_padded(padded, depth_len, width_len, long_len):
    summed = CENTER_WEIGHT * padded[..., 1 : 1 + depth_len, 1 : 1 + width_len, 1 : 1 + long_len]
    for off_depth in (-1, 0, 1):
        for off_width in (-1, 0, 1):
            for off_long in (-1, 0, 1):
                order_no = abs(off_depth) + abs(off_width) + abs(off_long)
                if order_no > 0:
                    summed = (
                        summed
                        - LAP_WEIGHTS[order_no]
                        * padded[
                            ...,
                            1 + off_depth : 1 + off_depth + depth_len,
                            1 + off_width : 1 + off_width + width_len,
                            1 + off_long : 1 + off_long + long_len,
                        ]
                    )
    return summed


def lateral_smooth(padded, width_len, long_len):
    summed = None
    for off_width in range(3):
        for off_long in range(3):
            weighted = (
                MASS_WEIGHTS[off_width]
                * MASS_WEIGHTS[off_long]
                * padded[..., off_width : off_width + width_len, off_long : off_long + long_len]
            )
            summed = weighted if summed is None else summed + weighted
    return summed


def plane_coupling(padded, width_len, long_len):
    summed = None
    for off_width in range(3):
        for off_long in range(3):
            order_no = 1 + (off_width != 1) + (off_long != 1)
            weighted = (
                LAP_WEIGHTS[order_no]
                * padded[..., off_width : off_width + width_len, off_long : off_long + long_len]
            )
            summed = weighted if summed is None else summed + weighted
    return summed


def combine_operator(negative, mass, damping):
    real_out = negative[:, 0] - WAVE_SCALE * (mass[:, 0] - damping * mass[:, 1])
    imag_out = negative[:, 1] - WAVE_SCALE * (mass[:, 1] + damping * mass[:, 0])
    return jnp.stack([real_out, imag_out], axis=1)


def inverse_diagonal(slowness, damping):
    scaled = WAVE_SCALE * MASS_WEIGHTS[1] * MASS_WEIGHTS[1] * slowness
    diag_re = LUMPED_DIAG - scaled * (1.0 + SHIFT_IMAG * damping)
    diag_im = -scaled * (damping + SHIFT_IMAG)
    norm_sq = diag_re * diag_re + diag_im * diag_im
    return (diag_re / norm_sq, -diag_im / norm_sq)


def complex_scale(inv_re, inv_im, values):
    real_part = values[:, 0]
    imag_part = values[:, 1]
    return jnp.stack(
        [inv_re * real_part - inv_im * imag_part, inv_re * imag_part + inv_im * real_part], axis=1
    )


def per_device(
    warm_field, slowness_sq, adjoint_field, observed, source_cell, receiver_cell, pml_width
):
    shot_count, _, layer_len, width_len, long_len = warm_field.shape
    depth_index = lax.axis_index("depth")
    tile_index = lax.axis_index("tile")
    depth_count = lax.axis_size("depth")
    tile_count = lax.axis_size("tile")
    full_depth = layer_len * depth_count
    full_width = width_len * tile_count
    depth_cells = depth_index * layer_len + jnp.arange(layer_len, dtype=jnp.int32)
    width_wide = (tile_index * width_len - 1 + jnp.arange(width_len + 2, dtype=jnp.int32)).astype(
        jnp.float32
    )
    damping_wide = damping_field(
        pml_width, depth_cells.astype(jnp.float32), width_wide, full_depth * 1.0, full_width * 1.0
    )[:, :, None]
    shots_here = shot_count // depth_count
    shot_start = depth_index * shots_here
    reach = -(-(full_depth - 1) // width_len)
    halo = reach * width_len
    window = width_len + 2 * halo

    def with_neighbour_rows(block):
        pieces = [shifted(block, "tile", step) for step in range(reach, 0, -1)]
        pieces.append(block)
        pieces += [shifted(block, "tile", -step) for step in range(1, reach + 1)]
        return jnp.concatenate(pieces, axis=-2)

    spread = jnp.broadcast_to(slowness_sq[None], (depth_count,) + slowness_sq.shape)
    slowness_all = lax.all_to_all(spread, "depth", 0, 1, tiled=True)[0]
    slowness_ext = with_neighbour_rows(slowness_all)
    rows_ext = tile_index * width_len - halo + jnp.arange(window, dtype=jnp.int32)
    damping_ext = damping_field(
        pml_width,
        jnp.arange(full_depth, dtype=jnp.float32),
        rows_ext.astype(jnp.float32),
        full_depth * 1.0,
        full_width * 1.0,
    )[:, :, None]
    inv_re, inv_im = inverse_diagonal(slowness_ext, damping_ext)
    row_valid = ((rows_ext >= 0) & (rows_ext < full_width))[:, None]

    def apply_window(values, slowness, damping, rows_out):
        padded = jnp.pad(values, [(0, 0), (0, 0), (1, 1), (0, 0), (1, 1)])
        negative = laplacian_from_padded(padded, full_depth, rows_out, long_len)
        mass = lateral_smooth(pad_long(values * slowness), rows_out, long_len)
        return combine_operator(negative, mass, damping)

    warm_t = lax.all_to_all(warm_field, "depth", 0, 2, tiled=True)
    warm_ext = with_neighbour_rows(warm_t)
    warm_pad = jnp.pad(warm_ext, [(0, 0), (0, 0), (0, 0), (1, 1), (0, 0)])
    slowness_pad = jnp.pad(slowness_ext, [(0, 0), (1, 1), (0, 0)])
    cell_index = (
        jnp.arange(full_depth, dtype=jnp.int32)[:, None, None] * full_width + rows_ext[None, :, None]
    ) * long_len + jnp.arange(long_len, dtype=jnp.int32)[None, None, :]
    my_sources = lax.dynamic_slice_in_dim(source_cell, shot_start, shots_here)
    hits = (cell_index[None] == my_sources[:, None, None, None]) & row_valid[None, None]
    source_re = jnp.where(hits, SOURCE_AMPLITUDE, 0.0).astype(jnp.float32)
    forcing = jnp.stack([source_re, jnp.zeros_like(source_re)], axis=1)
    residual_ext = forcing - apply_window(warm_pad, slowness_pad, damping_ext, window)

    def couple(plane_in):
        return plane_coupling(
            jnp.pad(plane_in, [(0, 0)] * (plane_in.ndim - 2) + [(1, 1), (1, 1)]),
            window,
            long_len,
        )

    previous = jnp.zeros((shots_here, 2, window, long_len), jnp.float32)
    layers_out = []
    for layer_no in range(full_depth):
        source_term = residual_ext[:, :, layer_no] + couple(previous)
        previous = jnp.where(
            row_valid, complex_scale(inv_re[layer_no], inv_im[layer_no], source_term), 0.0
        )
        layers_out.append(previous[:, :, halo : halo + width_len])
    downward_t = jnp.stack(layers_out, axis=2)
    downward_ext = with_neighbour_rows(downward_t)
    previous = jnp.zeros((shots_here, 2, window, long_len), jnp.float32)
    layers_out = [None] * full_depth
    for layer_no in range(full_depth - 1, -1, -1):
        previous = jnp.where(
            row_valid,
            downward_ext[:, :, layer_no]
            + complex_scale(inv_re[layer_no], inv_im[layer_no], couple(previous)),
            0.0,
        )
        layers_out[layer_no] = previous[:, :, halo - 1 : halo + width_len + 1]
    search_rim = jnp.stack(layers_out, axis=2)
    search_t = search_rim[:, :, :, 1:-1]
    image_field = apply_window(
        extended(search_t, (("tile", 3),), 1),
        slowness_ext[:, halo - 1 : halo + width_len + 1],
        damping_ext[:, halo : halo + width_len],
        width_len,
    )
    residual = residual_ext[:, :, :, halo : halo + width_len]
    local_real = jnp.sum(
        image_field[:, 0] * residual[:, 0] + image_field[:, 1] * residual[:, 1], axis=(1, 2, 3)
    )
    local_imag = jnp.sum(
        image_field[:, 0] * residual[:, 1] - image_field[:, 1] * residual[:, 0], axis=(1, 2, 3)
    )
    local_norm = jnp.sum(
        image_field[:, 0] * image_field[:, 0] + image_field[:, 1] * image_field[:, 1],
        axis=(1, 2, 3),
    )
    my_receivers = lax.dynamic_slice_in_dim(receiver_cell, shot_start, shots_here)
    my_observed = lax.dynamic_slice_in_dim(observed, shot_start, shots_here)
    plane_cells = full_width * long_len
    rec_depth = my_receivers // plane_cells
    rec_width = my_receivers // long_len % full_width
    rec_long = my_receivers % long_len
    local_width = rec_width - tile_index * width_len
    is_owned = (local_width >= 0) & (local_width < width_len)
    row_count = full_depth * width_len
    local_row = jnp.where(is_owned, rec_depth * width_len + local_width, -1)
    row_hot = (local_row[:, :, None] == jnp.arange(row_count, dtype=jnp.int32)).astype(jnp.float32)
    both_fields = jnp.concatenate([warm_t, search_t], axis=1).reshape(
        shots_here, 4, row_count, long_len
    )
    picked_rows = jnp.einsum(
        "srk,sqky->sqry", row_hot, both_fields, precision=lax.Precision.HIGHEST
    )
    col_hot = rec_long[:, None, :, None] == jnp.arange(long_len, dtype=jnp.int32)
    picked = jnp.sum(jnp.where(col_hot, picked_rows, 0.0), axis=-1)
    gap_re = picked[:, 0] - my_observed[:, 0]
    gap_im = picked[:, 1] - my_observed[:, 1]
    dir_re = picked[:, 2]
    dir_im = picked[:, 3]

    def owned_sum(values):
        return jnp.sum(jnp.where(is_owned, values, 0.0), axis=1)

    gap_norm = owned_sum(gap_re * gap_re + gap_im * gap_im)
    cross_re = owned_sum(gap_re * dir_re + gap_im * dir_im)
    cross_im = owned_sum(gap_re * dir_im - gap_im * dir_re)
    dir_norm = owned_sum(dir_re * dir_re + dir_im * dir_im)
    mine = jnp.stack(
        [local_real, local_imag, local_norm, gap_norm, cross_re, cross_im, dir_norm], axis=1
    )
    packed = lax.dynamic_update_slice_in_dim(
        jnp.zeros((shot_count, mine.shape[1]), jnp.float32), mine, shot_start, 0
    )
    packed = all_sum(packed)
    dot_real, dot_imag, image_norm = packed[:, 0], packed[:, 1], packed[:, 2]
    gap_norm, cross_re, cross_im, dir_norm = packed[:, 3], packed[:, 4], packed[:, 5], packed[:, 6]
    scale_re = dot_real / image_norm
    scale_im = dot_imag / image_norm
    step_re = lax.dynamic_slice_in_dim(scale_re, shot_start, shots_here)[:, None, None, None]
    step_im = lax.dynamic_slice_in_dim(scale_im, shot_start, shots_here)[:, None, None, None]
    new_re_t = warm_t[:, 0] + step_re * search_t[:, 0] - step_im * search_t[:, 1]
    new_im_t = warm_t[:, 1] + step_re * search_t[:, 1] + step_im * search_t[:, 0]
    new_field = lax.all_to_all(
        jnp.stack([new_re_t, new_im_t], axis=1), "depth", 2, 0, tiled=True
    )
    new_re = new_field[:, 0]
    new_im = new_field[:, 1]
    misfit = 0.5 * (
        gap_norm
        + 2.0 * (scale_re * cross_re - scale_im * cross_im)
        + (scale_re * scale_re + scale_im * scale_im) * dir_norm
    )
    adjoint_wide = extended(adjoint_field, (("tile", 3),), 1)
    adjoint_re = adjoint_wide[:, 0]
    adjoint_im = adjoint_wide[:, 1]
    weight_re = adjoint_re + damping_wide * adjoint_im
    weight_im = damping_wide * adjoint_re - adjoint_im
    smooth_re = lateral_smooth(pad_long(weight_re), width_len, long_len)
    smooth_im = lateral_smooth(pad_long(weight_im), width_len, long_len)
    gradient = -WAVE_SCALE / shot_count * jnp.sum(new_re * smooth_re - new_im * smooth_im, axis=0)
    return (new_field, misfit, gradient)


def solution(mesh):
    return jax.shard_map(
        per_device,
        mesh=mesh,
        in_specs=(
            P(None, None, "depth", "tile", None),
            P("depth", "tile", None),
            P(None, None, "depth", "tile", None),
            P(),
            P(),
            P(),
            P(),
        ),
        out_specs=(P(None, None, "depth", "tile", None), P(), P("depth", "tile", None)),
        check_vma=False,
    )
```

```python
import jax
import jax.numpy as jnp
from jax import lax
from jax.sharding import PartitionSpec as P
from jax.experimental import pallas as pl
from jax.experimental.pallas import tpu as pltpu
import functools

WAVE_SCALE = 1.9
PML_DAMP = 2.0
SOURCE_AMPLITUDE = 25.0
SHIFT_IMAG = 0.5
CENTER_WEIGHT = 128.0 / 30.0
LUMPED_DIAG = 2.0
LAP_WEIGHTS = (0.0, 14.0 / 30.0, 3.0 / 30.0, 1.0 / 30.0)
MASS_WEIGHTS = (1.0 / 6.0, 2.0 / 3.0, 1.0 / 6.0)


def extended(shard, sides, width):
    for axis, dim in sides:
        size, length = (lax.axis_size(axis), shard.shape[dim])
        up = [(i, (i + 1) % size) for i in range(size - 1)]
        down = [(j, i) for i, j in up]
        last = lax.slice_in_dim(shard, length - width, length, axis=dim)
        leading = lax.slice_in_dim(shard, 0, width, axis=dim)
        before = lax.ppermute(last, axis, up)
        after = lax.ppermute(leading, axis, down)
        shard = jnp.concatenate([before, shard, after], axis=dim)
    return shard


def shifted(value, axis, steps):
    count = lax.axis_size(axis)
    leading, last = (max(0, -steps), min(count, count - steps))
    return lax.ppermute(value, axis, [(source, source + steps) for source in range(leading, last)])


def all_sum_kernel(depth_count, tile_count, x_ref, out_ref, tile_slots, depth_slots, part,
                   copy_sem, tile_send, tile_recv, depth_send, depth_recv):
    me_d = lax.axis_index("depth")
    me_t = lax.axis_index("tile")
    mesh_ids = pl.DeviceIdType.MESH
    barrier = pltpu.get_barrier_semaphore()
    for k in range(1, tile_count):
        pl.semaphore_signal(barrier, inc=1, device_id=(me_d, lax.rem(me_t + k, tile_count)),
                            device_id_type=mesh_ids)
    for k in range(1, depth_count):
        pl.semaphore_signal(barrier, inc=1, device_id=(lax.rem(me_d + k, depth_count), me_t),
                            device_id_type=mesh_ids)
    pl.semaphore_wait(barrier, tile_count + depth_count - 2)

    def exchange(src, slots, send_sems, recv_sems, me, count, peer_of):
        own = pltpu.make_async_copy(src, slots.at[me], copy_sem)
        own.start()
        sends = []
        for k in range(1, count):
            copy = pltpu.make_async_remote_copy(
                src_ref=src, dst_ref=slots.at[me], send_sem=send_sems.at[k],
                recv_sem=recv_sems.at[me], device_id=peer_of(lax.rem(me + k, count)),
                device_id_type=mesh_ids)
            copy.start()
            sends.append(copy)
        own.wait()
        for k in range(1, count):
            sender = lax.rem(me + count - k, count)
            pltpu.make_async_remote_copy(
                src_ref=src, dst_ref=slots.at[sender], send_sem=send_sems.at[k],
                recv_sem=recv_sems.at[sender], device_id=peer_of(sender),
                device_id_type=mesh_ids).wait_recv()
        for copy in sends:
            copy.wait_send()
        total = slots[0]
        for j in range(1, count):
            total = total + slots[j]
        return total

    part[...] = exchange(x_ref, tile_slots, tile_send, tile_recv, me_t, tile_count,
                         lambda t: (me_d, t))
    out_ref[...] = exchange(part, depth_slots, depth_send, depth_recv, me_d, depth_count,
                            lambda d: (d, me_t))


def all_sum(values):
    depth_count = lax.axis_size("depth")
    tile_count = lax.axis_size("tile")
    size = values.size
    block = 128
    padded = -(-size // block) * block
    flat = jnp.pad(values.reshape(-1), (0, padded - size)).reshape(padded // 128, 128)
    summed = pl.pallas_call(
        functools.partial(all_sum_kernel, depth_count, tile_count),
        out_shape=jax.ShapeDtypeStruct(flat.shape, jnp.float32),
        in_specs=[pl.BlockSpec(memory_space=pltpu.VMEM)],
        out_specs=pl.BlockSpec(memory_space=pltpu.VMEM),
        scratch_shapes=[
            pltpu.VMEM((tile_count,) + flat.shape, jnp.float32),
            pltpu.VMEM((depth_count,) + flat.shape, jnp.float32),
            pltpu.VMEM(flat.shape, jnp.float32),
            pltpu.SemaphoreType.DMA,
            pltpu.SemaphoreType.DMA((tile_count,)),
            pltpu.SemaphoreType.DMA((tile_count,)),
            pltpu.SemaphoreType.DMA((depth_count,)),
            pltpu.SemaphoreType.DMA((depth_count,)),
        ],
        compiler_params=pltpu.CompilerParams(collective_id=0, has_side_effects=True),
    )(flat)
    return summed.reshape(-1)[:size].reshape(values.shape)


def damping_ramp(distance, extent):
    fraction = jnp.maximum((extent - distance) / extent, 0.0)
    return fraction * fraction


def damping_field(pml_width, depth_pos, width_pos, full_depth, full_width):
    widths = pml_width.astype(jnp.float32)
    depth_part = damping_ramp(depth_pos, widths[0]) + damping_ramp(
        full_depth - 1.0 - depth_pos, widths[1]
    )
    width_part = damping_ramp(width_pos, widths[2]) + damping_ramp(
        full_width - 1.0 - width_pos, widths[3]
    )
    return PML_DAMP * (depth_part[:, None] + width_part[None, :])


def pad_long(values):
    return jnp.pad(values, [(0, 0)] * (values.ndim - 1) + [(1, 1)])


def laplacian_from_padded(padded, depth_len, width_len, long_len):
    summed = CENTER_WEIGHT * padded[..., 1 : 1 + depth_len, 1 : 1 + width_len, 1 : 1 + long_len]
    for off_depth in (-1, 0, 1):
        for off_width in (-1, 0, 1):
            for off_long in (-1, 0, 1):
                order_no = abs(off_depth) + abs(off_width) + abs(off_long)
                if order_no > 0:
                    summed = (
                        summed
                        - LAP_WEIGHTS[order_no]
                        * padded[
                            ...,
                            1 + off_depth : 1 + off_depth + depth_len,
                            1 + off_width : 1 + off_width + width_len,
                            1 + off_long : 1 + off_long + long_len,
                        ]
                    )
    return summed


def lateral_smooth(padded, width_len, long_len):
    summed = None
    for off_width in range(3):
        for off_long in range(3):
            weighted = (
                MASS_WEIGHTS[off_width]
                * MASS_WEIGHTS[off_long]
                * padded[..., off_width : off_width + width_len, off_long : off_long + long_len]
            )
            summed = weighted if summed is None else summed + weighted
    return summed


def plane_coupling(padded, width_len, long_len):
    summed = None
    for off_width in range(3):
        for off_long in range(3):
            order_no = 1 + (off_width != 1) + (off_long != 1)
            weighted = (
                LAP_WEIGHTS[order_no]
                * padded[..., off_width : off_width + width_len, off_long : off_long + long_len]
            )
            summed = weighted if summed is None else summed + weighted
    return summed


def combine_operator(negative, mass, damping):
    real_out = negative[:, 0] - WAVE_SCALE * (mass[:, 0] - damping * mass[:, 1])
    imag_out = negative[:, 1] - WAVE_SCALE * (mass[:, 1] + damping * mass[:, 0])
    return jnp.stack([real_out, imag_out], axis=1)


def inverse_diagonal(slowness, damping):
    scaled = WAVE_SCALE * MASS_WEIGHTS[1] * MASS_WEIGHTS[1] * slowness
    diag_re = LUMPED_DIAG - scaled * (1.0 + SHIFT_IMAG * damping)
    diag_im = -scaled * (damping + SHIFT_IMAG)
    norm_sq = diag_re * diag_re + diag_im * diag_im
    return (diag_re / norm_sq, -diag_im / norm_sq)


def complex_scale(inv_re, inv_im, values):
    real_part = values[:, 0]
    imag_part = values[:, 1]
    return jnp.stack(
        [inv_re * real_part - inv_im * imag_part, inv_re * imag_part + inv_im * real_part], axis=1
    )


def per_device(
    warm_field, slowness_sq, adjoint_field, observed, source_cell, receiver_cell, pml_width
):
    shot_count, _, layer_len, width_len, long_len = warm_field.shape
    depth_index = lax.axis_index("depth")
    tile_index = lax.axis_index("tile")
    depth_count = lax.axis_size("depth")
    tile_count = lax.axis_size("tile")
    full_depth = layer_len * depth_count
    full_width = width_len * tile_count
    depth_cells = depth_index * layer_len + jnp.arange(layer_len, dtype=jnp.int32)
    width_cells = tile_index * width_len + jnp.arange(width_len, dtype=jnp.int32)
    width_wide = (tile_index * width_len - 1 + jnp.arange(width_len + 2, dtype=jnp.int32)).astype(
        jnp.float32
    )
    damping_wide = damping_field(
        pml_width, depth_cells.astype(jnp.float32), width_wide, full_depth * 1.0, full_width * 1.0
    )[:, :, None]
    damping = damping_wide[:, 1:-1]
    slowness_wide = extended(slowness_sq, (("tile", 1),), 1)

    def apply_operator(values):
        padded = extended(values, (("depth", 2), ("tile", 3)), 1)
        negative = laplacian_from_padded(pad_long(padded), layer_len, width_len, long_len)
        mass = lateral_smooth(pad_long(padded[:, :, 1:-1] * slowness_wide), width_len, long_len)
        return combine_operator(negative, mass, damping)

    cell_index = (
        depth_cells[:, None, None] * full_width + width_cells[None, :, None]
    ) * long_len + jnp.arange(long_len, dtype=jnp.int32)[None, None, :]
    hits = cell_index[None] == source_cell[:, None, None, None]
    source_re = jnp.where(hits, SOURCE_AMPLITUDE, 0.0).astype(jnp.float32)
    forcing = jnp.stack([source_re, jnp.zeros_like(source_re)], axis=1)
    residual = forcing - apply_operator(warm_field)

    shots_here = shot_count // depth_count
    reach = -(-(full_depth - 1) // width_len)
    halo = reach * width_len
    window = width_len + 2 * halo

    def with_neighbour_rows(block):
        pieces = [shifted(block, "tile", step) for step in range(reach, 0, -1)]
        pieces.append(block)
        pieces += [shifted(block, "tile", -step) for step in range(1, reach + 1)]
        return jnp.concatenate(pieces, axis=-2)

    spread = jnp.broadcast_to(slowness_sq[None], (depth_count,) + slowness_sq.shape)
    slowness_all = lax.all_to_all(spread, "depth", 0, 1, tiled=True)[0]
    slowness_ext = with_neighbour_rows(slowness_all)
    rows_ext = tile_index * width_len - halo + jnp.arange(window, dtype=jnp.int32)
    damping_ext = damping_field(
        pml_width,
        jnp.arange(full_depth, dtype=jnp.float32),
        rows_ext.astype(jnp.float32),
        full_depth * 1.0,
        full_width * 1.0,
    )[:, :, None]
    inv_re, inv_im = inverse_diagonal(slowness_ext, damping_ext)
    row_valid = ((rows_ext >= 0) & (rows_ext < full_width))[:, None]

    def couple(plane_in):
        return plane_coupling(
            jnp.pad(plane_in, [(0, 0)] * (plane_in.ndim - 2) + [(1, 1), (1, 1)]),
            window,
            long_len,
        )

    residual_t = lax.all_to_all(residual, "depth", 0, 2, tiled=True)
    residual_ext = with_neighbour_rows(residual_t)
    previous = jnp.zeros((shots_here, 2, window, long_len), jnp.float32)
    layers_out = []
    for layer_no in range(full_depth):
        source_term = residual_ext[:, :, layer_no] + couple(previous)
        previous = jnp.where(
            row_valid, complex_scale(inv_re[layer_no], inv_im[layer_no], source_term), 0.0
        )
        layers_out.append(previous[:, :, halo : halo + width_len])
    downward_t = jnp.stack(layers_out, axis=2)
    downward_ext = with_neighbour_rows(downward_t)
    previous = jnp.zeros((shots_here, 2, window, long_len), jnp.float32)
    layers_out = [None] * full_depth
    for layer_no in range(full_depth - 1, -1, -1):
        previous = jnp.where(
            row_valid,
            downward_ext[:, :, layer_no]
            + complex_scale(inv_re[layer_no], inv_im[layer_no], couple(previous)),
            0.0,
        )
        layers_out[layer_no] = previous[:, :, halo : halo + width_len]
    search_t = jnp.stack(layers_out, axis=2)
    search = lax.all_to_all(search_t, "depth", 2, 0, tiled=True)
    image_field = apply_operator(search)
    local_real = jnp.sum(
        image_field[:, 0] * residual[:, 0] + image_field[:, 1] * residual[:, 1], axis=(1, 2, 3)
    )
    local_imag = jnp.sum(
        image_field[:, 0] * residual[:, 1] - image_field[:, 1] * residual[:, 0], axis=(1, 2, 3)
    )
    local_norm = jnp.sum(
        image_field[:, 0] * image_field[:, 0] + image_field[:, 1] * image_field[:, 1],
        axis=(1, 2, 3),
    )
    plane_cells = full_width * long_len
    rec_depth = receiver_cell // plane_cells
    rec_width = receiver_cell // long_len % full_width
    rec_long = receiver_cell % long_len
    local_depth = rec_depth - depth_index * layer_len
    local_width = rec_width - tile_index * width_len
    is_owned = (
        (local_depth >= 0)
        & (local_depth < layer_len)
        & (local_width >= 0)
        & (local_width < width_len)
    )
    row_count = layer_len * width_len
    local_row = jnp.where(is_owned, local_depth * width_len + local_width, -1)
    row_hot = (local_row[:, :, None] == jnp.arange(row_count, dtype=jnp.int32)).astype(jnp.float32)
    both_fields = jnp.concatenate([warm_field, search], axis=1).reshape(
        shot_count, 4, row_count, long_len
    )
    picked_rows = jnp.einsum(
        "srk,sqky->sqry", row_hot, both_fields, precision=lax.Precision.HIGHEST
    )
    col_hot = rec_long[:, None, :, None] == jnp.arange(long_len, dtype=jnp.int32)
    picked = jnp.sum(jnp.where(col_hot, picked_rows, 0.0), axis=-1)
    gap_re = picked[:, 0] - observed[:, 0]
    gap_im = picked[:, 1] - observed[:, 1]
    dir_re = picked[:, 2]
    dir_im = picked[:, 3]

    def owned_sum(values):
        return jnp.sum(jnp.where(is_owned, values, 0.0), axis=1)

    gap_norm = owned_sum(gap_re * gap_re + gap_im * gap_im)
    cross_re = owned_sum(gap_re * dir_re + gap_im * dir_im)
    cross_im = owned_sum(gap_re * dir_im - gap_im * dir_re)
    dir_norm = owned_sum(dir_re * dir_re + dir_im * dir_im)
    packed = jnp.stack(
        [local_real, local_imag, local_norm, gap_norm, cross_re, cross_im, dir_norm], axis=1
    )
    packed = all_sum(packed)
    dot_real, dot_imag, image_norm = packed[:, 0], packed[:, 1], packed[:, 2]
    gap_norm, cross_re, cross_im, dir_norm = packed[:, 3], packed[:, 4], packed[:, 5], packed[:, 6]
    step_re = (dot_real / image_norm)[:, None, None, None]
    step_im = (dot_imag / image_norm)[:, None, None, None]
    new_re = warm_field[:, 0] + step_re * search[:, 0] - step_im * search[:, 1]
    new_im = warm_field[:, 1] + step_re * search[:, 1] + step_im * search[:, 0]
    new_field = jnp.stack([new_re, new_im], axis=1)
    scale_re = dot_real / image_norm
    scale_im = dot_imag / image_norm
    misfit = 0.5 * (
        gap_norm
        + 2.0 * (scale_re * cross_re - scale_im * cross_im)
        + (scale_re * scale_re + scale_im * scale_im) * dir_norm
    )
    adjoint_wide = extended(adjoint_field, (("tile", 3),), 1)
    adjoint_re = adjoint_wide[:, 0]
    adjoint_im = adjoint_wide[:, 1]
    weight_re = adjoint_re + damping_wide * adjoint_im
    weight_im = damping_wide * adjoint_re - adjoint_im
    smooth_re = lateral_smooth(pad_long(weight_re), width_len, long_len)
    smooth_im = lateral_smooth(pad_long(weight_im), width_len, long_len)
    gradient = -WAVE_SCALE / shot_count * jnp.sum(new_re * smooth_re - new_im * smooth_im, axis=0)
    return (new_field, misfit, gradient)


def solution(mesh):
    return jax.shard_map(
        per_device,
        mesh=mesh,
        in_specs=(
            P(None, None, "depth", "tile", None),
            P("depth", "tile", None),
            P(None, None, "depth", "tile", None),
            P(),
            P(),
            P(),
            P(),
        ),
        out_specs=(P(None, None, "depth", "tile", None), P(), P("depth", "tile", None)),
        check_vma=False,
    )
```

```python
import jax
import jax.numpy as jnp
from jax import lax
from jax.sharding import PartitionSpec as P
from jax.experimental import pallas as pl
from jax.experimental.pallas import tpu as pltpu
import functools

WAVE_SCALE = 1.9
PML_DAMP = 2.0
SOURCE_AMPLITUDE = 25.0
SHIFT_IMAG = 0.5
CENTER_WEIGHT = 128.0 / 30.0
LUMPED_DIAG = 2.0
LAP_WEIGHTS = (0.0, 14.0 / 30.0, 3.0 / 30.0, 1.0 / 30.0)
MASS_WEIGHTS = (1.0 / 6.0, 2.0 / 3.0, 1.0 / 6.0)


def extended(shard, sides, width):
    for axis, dim in sides:
        size, length = (lax.axis_size(axis), shard.shape[dim])
        up = [(i, (i + 1) % size) for i in range(size - 1)]
        down = [(j, i) for i, j in up]
        last = lax.slice_in_dim(shard, length - width, length, axis=dim)
        leading = lax.slice_in_dim(shard, 0, width, axis=dim)
        before = lax.ppermute(last, axis, up)
        after = lax.ppermute(leading, axis, down)
        shard = jnp.concatenate([before, shard, after], axis=dim)
    return shard


def shifted(value, axis, steps):
    count = lax.axis_size(axis)
    leading, last = (max(0, -steps), min(count, count - steps))
    return lax.ppermute(value, axis, [(source, source + steps) for source in range(leading, last)])


def all_sum_kernel(depth_count, tile_count, x_ref, out_ref, tile_slots, depth_slots, part,
                   copy_sem, tile_send, tile_recv, depth_send, depth_recv):
    me_d = lax.axis_index("depth")
    me_t = lax.axis_index("tile")
    mesh_ids = pl.DeviceIdType.MESH
    barrier = pltpu.get_barrier_semaphore()
    for k in range(1, tile_count):
        pl.semaphore_signal(barrier, inc=1, device_id=(me_d, lax.rem(me_t + k, tile_count)),
                            device_id_type=mesh_ids)
    for k in range(1, depth_count):
        pl.semaphore_signal(barrier, inc=1, device_id=(lax.rem(me_d + k, depth_count), me_t),
                            device_id_type=mesh_ids)
    pl.semaphore_wait(barrier, tile_count + depth_count - 2)

    def exchange(src, slots, send_sems, recv_sems, me, count, peer_of):
        own = pltpu.make_async_copy(src, slots.at[me], copy_sem)
        own.start()
        sends = []
        for k in range(1, count):
            copy = pltpu.make_async_remote_copy(
                src_ref=src, dst_ref=slots.at[me], send_sem=send_sems.at[k],
                recv_sem=recv_sems.at[me], device_id=peer_of(lax.rem(me + k, count)),
                device_id_type=mesh_ids)
            copy.start()
            sends.append(copy)
        own.wait()
        for k in range(1, count):
            sender = lax.rem(me + count - k, count)
            pltpu.make_async_remote_copy(
                src_ref=src, dst_ref=slots.at[sender], send_sem=send_sems.at[k],
                recv_sem=recv_sems.at[sender], device_id=peer_of(sender),
                device_id_type=mesh_ids).wait_recv()
        for copy in sends:
            copy.wait_send()
        total = slots[0]
        for j in range(1, count):
            total = total + slots[j]
        return total

    part[...] = exchange(x_ref, tile_slots, tile_send, tile_recv, me_t, tile_count,
                         lambda t: (me_d, t))
    out_ref[...] = exchange(part, depth_slots, depth_send, depth_recv, me_d, depth_count,
                            lambda d: (d, me_t))


def all_sum(values):
    depth_count = lax.axis_size("depth")
    tile_count = lax.axis_size("tile")
    size = values.size
    block = 128
    padded = -(-size // block) * block
    flat = jnp.pad(values.reshape(-1), (0, padded - size)).reshape(padded // 128, 128)
    summed = pl.pallas_call(
        functools.partial(all_sum_kernel, depth_count, tile_count),
        out_shape=jax.ShapeDtypeStruct(flat.shape, jnp.float32),
        in_specs=[pl.BlockSpec(memory_space=pltpu.VMEM)],
        out_specs=pl.BlockSpec(memory_space=pltpu.VMEM),
        scratch_shapes=[
            pltpu.VMEM((tile_count,) + flat.shape, jnp.float32),
            pltpu.VMEM((depth_count,) + flat.shape, jnp.float32),
            pltpu.VMEM(flat.shape, jnp.float32),
            pltpu.SemaphoreType.DMA,
            pltpu.SemaphoreType.DMA((tile_count,)),
            pltpu.SemaphoreType.DMA((tile_count,)),
            pltpu.SemaphoreType.DMA((depth_count,)),
            pltpu.SemaphoreType.DMA((depth_count,)),
        ],
        compiler_params=pltpu.CompilerParams(collective_id=0, has_side_effects=True),
    )(flat)
    return summed.reshape(-1)[:size].reshape(values.shape)


def damping_ramp(distance, extent):
    fraction = jnp.maximum((extent - distance) / extent, 0.0)
    return fraction * fraction


def damping_field(pml_width, depth_pos, width_pos, full_depth, full_width):
    widths = pml_width.astype(jnp.float32)
    depth_part = damping_ramp(depth_pos, widths[0]) + damping_ramp(
        full_depth - 1.0 - depth_pos, widths[1]
    )
    width_part = damping_ramp(width_pos, widths[2]) + damping_ramp(
        full_width - 1.0 - width_pos, widths[3]
    )
    return PML_DAMP * (depth_part[:, None] + width_part[None, :])


def pad_long(values):
    return jnp.pad(values, [(0, 0)] * (values.ndim - 1) + [(1, 1)])


def laplacian_from_padded(padded, depth_len, width_len, long_len):
    summed = CENTER_WEIGHT * padded[..., 1 : 1 + depth_len, 1 : 1 + width_len, 1 : 1 + long_len]
    for off_depth in (-1, 0, 1):
        for off_width in (-1, 0, 1):
            for off_long in (-1, 0, 1):
                order_no = abs(off_depth) + abs(off_width) + abs(off_long)
                if order_no > 0:
                    summed = (
                        summed
                        - LAP_WEIGHTS[order_no]
                        * padded[
                            ...,
                            1 + off_depth : 1 + off_depth + depth_len,
                            1 + off_width : 1 + off_width + width_len,
                            1 + off_long : 1 + off_long + long_len,
                        ]
                    )
    return summed


def lateral_smooth(padded, width_len, long_len):
    summed = None
    for off_width in range(3):
        for off_long in range(3):
            weighted = (
                MASS_WEIGHTS[off_width]
                * MASS_WEIGHTS[off_long]
                * padded[..., off_width : off_width + width_len, off_long : off_long + long_len]
            )
            summed = weighted if summed is None else summed + weighted
    return summed


def plane_coupling(padded, width_len, long_len):
    summed = None
    for off_width in range(3):
        for off_long in range(3):
            order_no = 1 + (off_width != 1) + (off_long != 1)
            weighted = (
                LAP_WEIGHTS[order_no]
                * padded[..., off_width : off_width + width_len, off_long : off_long + long_len]
            )
            summed = weighted if summed is None else summed + weighted
    return summed


def combine_operator(negative, mass, damping):
    real_out = negative[:, 0] - WAVE_SCALE * (mass[:, 0] - damping * mass[:, 1])
    imag_out = negative[:, 1] - WAVE_SCALE * (mass[:, 1] + damping * mass[:, 0])
    return jnp.stack([real_out, imag_out], axis=1)


def inverse_diagonal(slowness, damping):
    scaled = WAVE_SCALE * MASS_WEIGHTS[1] * MASS_WEIGHTS[1] * slowness
    diag_re = LUMPED_DIAG - scaled * (1.0 + SHIFT_IMAG * damping)
    diag_im = -scaled * (damping + SHIFT_IMAG)
    norm_sq = diag_re * diag_re + diag_im * diag_im
    return (diag_re / norm_sq, -diag_im / norm_sq)


def complex_scale(inv_re, inv_im, values):
    real_part = values[:, 0]
    imag_part = values[:, 1]
    return jnp.stack(
        [inv_re * real_part - inv_im * imag_part, inv_re * imag_part + inv_im * real_part], axis=1
    )


def per_device(
    warm_field, slowness_sq, adjoint_field, observed, source_cell, receiver_cell, pml_width
):
    shot_count, _, layer_len, width_len, long_len = warm_field.shape
    depth_index = lax.axis_index("depth")
    tile_index = lax.axis_index("tile")
    depth_count = lax.axis_size("depth")
    tile_count = lax.axis_size("tile")
    full_depth = layer_len * depth_count
    full_width = width_len * tile_count
    depth_cells = depth_index * layer_len + jnp.arange(layer_len, dtype=jnp.int32)
    width_cells = tile_index * width_len + jnp.arange(width_len, dtype=jnp.int32)
    width_wide = (tile_index * width_len - 1 + jnp.arange(width_len + 2, dtype=jnp.int32)).astype(
        jnp.float32
    )
    damping_wide = damping_field(
        pml_width, depth_cells.astype(jnp.float32), width_wide, full_depth * 1.0, full_width * 1.0
    )[:, :, None]
    damping = damping_wide[:, 1:-1]
    slowness_wide = extended(slowness_sq, (("tile", 1),), 1)

    def apply_operator(values):
        padded = extended(values, (("depth", 2), ("tile", 3)), 1)
        negative = laplacian_from_padded(pad_long(padded), layer_len, width_len, long_len)
        mass = lateral_smooth(pad_long(padded[:, :, 1:-1] * slowness_wide), width_len, long_len)
        return combine_operator(negative, mass, damping)

    cell_index = (
        depth_cells[:, None, None] * full_width + width_cells[None, :, None]
    ) * long_len + jnp.arange(long_len, dtype=jnp.int32)[None, None, :]
    hits = cell_index[None] == source_cell[:, None, None, None]
    source_re = jnp.where(hits, SOURCE_AMPLITUDE, 0.0).astype(jnp.float32)
    forcing = jnp.stack([source_re, jnp.zeros_like(source_re)], axis=1)
    residual = forcing - apply_operator(warm_field)

    shots_here = shot_count // depth_count
    reach = -(-(full_depth - 1) // width_len)
    halo = reach * width_len
    window = width_len + 2 * halo

    def with_neighbour_rows(block):
        pieces = [shifted(block, "tile", step) for step in range(reach, 0, -1)]
        pieces.append(block)
        pieces += [shifted(block, "tile", -step) for step in range(1, reach + 1)]
        return jnp.concatenate(pieces, axis=-2)

    spread = jnp.broadcast_to(slowness_sq[None], (depth_count,) + slowness_sq.shape)
    slowness_all = lax.all_to_all(spread, "depth", 0, 1, tiled=True)[0]
    slowness_ext = with_neighbour_rows(slowness_all)
    rows_ext = tile_index * width_len - halo + jnp.arange(window, dtype=jnp.int32)
    damping_ext = damping_field(
        pml_width,
        jnp.arange(full_depth, dtype=jnp.float32),
        rows_ext.astype(jnp.float32),
        full_depth * 1.0,
        full_width * 1.0,
    )[:, :, None]
    inv_re, inv_im = inverse_diagonal(slowness_ext, damping_ext)
    row_valid = ((rows_ext >= 0) & (rows_ext < full_width))[:, None]

    def couple(plane_in):
        return plane_coupling(
            jnp.pad(plane_in, [(0, 0)] * (plane_in.ndim - 2) + [(1, 1), (1, 1)]),
            window,
            long_len,
        )

    residual_t = lax.all_to_all(residual, "depth", 0, 2, tiled=True)
    residual_ext = with_neighbour_rows(residual_t)
    previous = jnp.zeros((shots_here, 2, window, long_len), jnp.float32)
    layers_out = []
    for layer_no in range(full_depth):
        source_term = residual_ext[:, :, layer_no] + couple(previous)
        previous = jnp.where(
            row_valid, complex_scale(inv_re[layer_no], inv_im[layer_no], source_term), 0.0
        )
        layers_out.append(previous)
    cut = min(halo // 2 + 1, full_depth)
    downward_ext = jnp.stack(layers_out, axis=2)
    if cut < full_depth:
        late = with_neighbour_rows(downward_ext[:, :, cut:, halo : halo + width_len])
        downward_ext = jnp.concatenate([downward_ext[:, :, :cut], late], axis=2)
    previous = jnp.zeros((shots_here, 2, window, long_len), jnp.float32)
    layers_out = [None] * full_depth
    for layer_no in range(full_depth - 1, -1, -1):
        previous = jnp.where(
            row_valid,
            downward_ext[:, :, layer_no]
            + complex_scale(inv_re[layer_no], inv_im[layer_no], couple(previous)),
            0.0,
        )
        layers_out[layer_no] = previous[:, :, halo : halo + width_len]
    search_t = jnp.stack(layers_out, axis=2)
    search = lax.all_to_all(search_t, "depth", 2, 0, tiled=True)
    image_field = apply_operator(search)
    local_real = jnp.sum(
        image_field[:, 0] * residual[:, 0] + image_field[:, 1] * residual[:, 1], axis=(1, 2, 3)
    )
    local_imag = jnp.sum(
        image_field[:, 0] * residual[:, 1] - image_field[:, 1] * residual[:, 0], axis=(1, 2, 3)
    )
    local_norm = jnp.sum(
        image_field[:, 0] * image_field[:, 0] + image_field[:, 1] * image_field[:, 1],
        axis=(1, 2, 3),
    )
    plane_cells = full_width * long_len
    rec_depth = receiver_cell // plane_cells
    rec_width = receiver_cell // long_len % full_width
    rec_long = receiver_cell % long_len
    local_depth = rec_depth - depth_index * layer_len
    local_width = rec_width - tile_index * width_len
    is_owned = (
        (local_depth >= 0)
        & (local_depth < layer_len)
        & (local_width >= 0)
        & (local_width < width_len)
    )
    row_count = layer_len * width_len
    local_row = jnp.where(is_owned, local_depth * width_len + local_width, -1)
    row_hot = (local_row[:, :, None] == jnp.arange(row_count, dtype=jnp.int32)).astype(jnp.float32)
    both_fields = jnp.concatenate([warm_field, search], axis=1).reshape(
        shot_count, 4, row_count, long_len
    )
    picked_rows = jnp.einsum(
        "srk,sqky->sqry", row_hot, both_fields, precision=lax.Precision.HIGHEST
    )
    col_hot = rec_long[:, None, :, None] == jnp.arange(long_len, dtype=jnp.int32)
    picked = jnp.sum(jnp.where(col_hot, picked_rows, 0.0), axis=-1)
    gap_re = picked[:, 0] - observed[:, 0]
    gap_im = picked[:, 1] - observed[:, 1]
    dir_re = picked[:, 2]
    dir_im = picked[:, 3]

    def owned_sum(values):
        return jnp.sum(jnp.where(is_owned, values, 0.0), axis=1)

    gap_norm = owned_sum(gap_re * gap_re + gap_im * gap_im)
    cross_re = owned_sum(gap_re * dir_re + gap_im * dir_im)
    cross_im = owned_sum(gap_re * dir_im - gap_im * dir_re)
    dir_norm = owned_sum(dir_re * dir_re + dir_im * dir_im)
    packed = jnp.stack(
        [local_real, local_imag, local_norm, gap_norm, cross_re, cross_im, dir_norm], axis=1
    )
    packed = all_sum(packed)
    dot_real, dot_imag, image_norm = packed[:, 0], packed[:, 1], packed[:, 2]
    gap_norm, cross_re, cross_im, dir_norm = packed[:, 3], packed[:, 4], packed[:, 5], packed[:, 6]
    step_re = (dot_real / image_norm)[:, None, None, None]
    step_im = (dot_imag / image_norm)[:, None, None, None]
    new_re = warm_field[:, 0] + step_re * search[:, 0] - step_im * search[:, 1]
    new_im = warm_field[:, 1] + step_re * search[:, 1] + step_im * search[:, 0]
    new_field = jnp.stack([new_re, new_im], axis=1)
    scale_re = dot_real / image_norm
    scale_im = dot_imag / image_norm
    misfit = 0.5 * (
        gap_norm
        + 2.0 * (scale_re * cross_re - scale_im * cross_im)
        + (scale_re * scale_re + scale_im * scale_im) * dir_norm
    )
    adjoint_wide = extended(adjoint_field, (("tile", 3),), 1)
    adjoint_re = adjoint_wide[:, 0]
    adjoint_im = adjoint_wide[:, 1]
    weight_re = adjoint_re + damping_wide * adjoint_im
    weight_im = damping_wide * adjoint_re - adjoint_im
    smooth_re = lateral_smooth(pad_long(weight_re), width_len, long_len)
    smooth_im = lateral_smooth(pad_long(weight_im), width_len, long_len)
    gradient = -WAVE_SCALE / shot_count * jnp.sum(new_re * smooth_re - new_im * smooth_im, axis=0)
    return (new_field, misfit, gradient)


def solution(mesh):
    return jax.shard_map(
        per_device,
        mesh=mesh,
        in_specs=(
            P(None, None, "depth", "tile", None),
            P("depth", "tile", None),
            P(None, None, "depth", "tile", None),
            P(),
            P(),
            P(),
            P(),
        ),
        out_specs=(P(None, None, "depth", "tile", None), P(), P("depth", "tile", None)),
        check_vma=False,
    )
```

```python
import jax
import jax.numpy as jnp
from jax import lax
from jax.sharding import PartitionSpec as P
from jax.experimental import pallas as pl
from jax.experimental.pallas import tpu as pltpu
import functools

WAVE_SCALE = 1.9
PML_DAMP = 2.0
SOURCE_AMPLITUDE = 25.0
SHIFT_IMAG = 0.5
CENTER_WEIGHT = 128.0 / 30.0
LUMPED_DIAG = 2.0
LAP_WEIGHTS = (0.0, 14.0 / 30.0, 3.0 / 30.0, 1.0 / 30.0)
MASS_WEIGHTS = (1.0 / 6.0, 2.0 / 3.0, 1.0 / 6.0)


def extended(shard, sides, width):
    for axis, dim in sides:
        size, length = (lax.axis_size(axis), shard.shape[dim])
        up = [(i, (i + 1) % size) for i in range(size - 1)]
        down = [(j, i) for i, j in up]
        last = lax.slice_in_dim(shard, length - width, length, axis=dim)
        leading = lax.slice_in_dim(shard, 0, width, axis=dim)
        before = lax.ppermute(last, axis, up)
        after = lax.ppermute(leading, axis, down)
        shard = jnp.concatenate([before, shard, after], axis=dim)
    return shard


def shifted(value, axis, steps):
    count = lax.axis_size(axis)
    leading, last = (max(0, -steps), min(count, count - steps))
    return lax.ppermute(value, axis, [(source, source + steps) for source in range(leading, last)])


def all_sum_kernel(depth_count, tile_count, x_ref, out_ref, tile_slots, depth_slots, part,
                   copy_sem, tile_send, tile_recv, depth_send, depth_recv):
    me_d = lax.axis_index("depth")
    me_t = lax.axis_index("tile")
    mesh_ids = pl.DeviceIdType.MESH
    barrier = pltpu.get_barrier_semaphore()
    for k in range(1, tile_count):
        pl.semaphore_signal(barrier, inc=1, device_id=(me_d, lax.rem(me_t + k, tile_count)),
                            device_id_type=mesh_ids)
    for k in range(1, depth_count):
        pl.semaphore_signal(barrier, inc=1, device_id=(lax.rem(me_d + k, depth_count), me_t),
                            device_id_type=mesh_ids)
    pl.semaphore_wait(barrier, tile_count + depth_count - 2)

    def exchange(src, slots, send_sems, recv_sems, me, count, peer_of):
        own = pltpu.make_async_copy(src, slots.at[me], copy_sem)
        own.start()
        sends = []
        for k in range(1, count):
            copy = pltpu.make_async_remote_copy(
                src_ref=src, dst_ref=slots.at[me], send_sem=send_sems.at[k],
                recv_sem=recv_sems.at[me], device_id=peer_of(lax.rem(me + k, count)),
                device_id_type=mesh_ids)
            copy.start()
            sends.append(copy)
        own.wait()
        for k in range(1, count):
            sender = lax.rem(me + count - k, count)
            pltpu.make_async_remote_copy(
                src_ref=src, dst_ref=slots.at[sender], send_sem=send_sems.at[k],
                recv_sem=recv_sems.at[sender], device_id=peer_of(sender),
                device_id_type=mesh_ids).wait_recv()
        for copy in sends:
            copy.wait_send()
        total = slots[0]
        for j in range(1, count):
            total = total + slots[j]
        return total

    part[...] = exchange(x_ref, tile_slots, tile_send, tile_recv, me_t, tile_count,
                         lambda t: (me_d, t))
    out_ref[...] = exchange(part, depth_slots, depth_send, depth_recv, me_d, depth_count,
                            lambda d: (d, me_t))


def all_sum(values):
    depth_count = lax.axis_size("depth")
    tile_count = lax.axis_size("tile")
    size = values.size
    block = 128
    padded = -(-size // block) * block
    flat = jnp.pad(values.reshape(-1), (0, padded - size)).reshape(padded // 128, 128)
    summed = pl.pallas_call(
        functools.partial(all_sum_kernel, depth_count, tile_count),
        out_shape=jax.ShapeDtypeStruct(flat.shape, jnp.float32),
        in_specs=[pl.BlockSpec(memory_space=pltpu.VMEM)],
        out_specs=pl.BlockSpec(memory_space=pltpu.VMEM),
        scratch_shapes=[
            pltpu.VMEM((tile_count,) + flat.shape, jnp.float32),
            pltpu.VMEM((depth_count,) + flat.shape, jnp.float32),
            pltpu.VMEM(flat.shape, jnp.float32),
            pltpu.SemaphoreType.DMA,
            pltpu.SemaphoreType.DMA((tile_count,)),
            pltpu.SemaphoreType.DMA((tile_count,)),
            pltpu.SemaphoreType.DMA((depth_count,)),
            pltpu.SemaphoreType.DMA((depth_count,)),
        ],
        compiler_params=pltpu.CompilerParams(collective_id=0, has_side_effects=True),
    )(flat)
    return summed.reshape(-1)[:size].reshape(values.shape)


def damping_ramp(distance, extent):
    fraction = jnp.maximum((extent - distance) / extent, 0.0)
    return fraction * fraction


def damping_field(pml_width, depth_pos, width_pos, full_depth, full_width):
    widths = pml_width.astype(jnp.float32)
    depth_part = damping_ramp(depth_pos, widths[0]) + damping_ramp(
        full_depth - 1.0 - depth_pos, widths[1]
    )
    width_part = damping_ramp(width_pos, widths[2]) + damping_ramp(
        full_width - 1.0 - width_pos, widths[3]
    )
    return PML_DAMP * (depth_part[:, None] + width_part[None, :])


def pad_long(values):
    return jnp.pad(values, [(0, 0)] * (values.ndim - 1) + [(1, 1)])


def laplacian_from_padded(padded, depth_len, width_len, long_len):
    summed = CENTER_WEIGHT * padded[..., 1 : 1 + depth_len, 1 : 1 + width_len, 1 : 1 + long_len]
    for off_depth in (-1, 0, 1):
        for off_width in (-1, 0, 1):
            for off_long in (-1, 0, 1):
                order_no = abs(off_depth) + abs(off_width) + abs(off_long)
                if order_no > 0:
                    summed = (
                        summed
                        - LAP_WEIGHTS[order_no]
                        * padded[
                            ...,
                            1 + off_depth : 1 + off_depth + depth_len,
                            1 + off_width : 1 + off_width + width_len,
                            1 + off_long : 1 + off_long + long_len,
                        ]
                    )
    return summed


def lateral_smooth(padded, width_len, long_len):
    summed = None
    for off_width in range(3):
        for off_long in range(3):
            weighted = (
                MASS_WEIGHTS[off_width]
                * MASS_WEIGHTS[off_long]
                * padded[..., off_width : off_width + width_len, off_long : off_long + long_len]
            )
            summed = weighted if summed is None else summed + weighted
    return summed


def plane_coupling(padded, width_len, long_len):
    summed = None
    for off_width in range(3):
        for off_long in range(3):
            order_no = 1 + (off_width != 1) + (off_long != 1)
            weighted = (
                LAP_WEIGHTS[order_no]
                * padded[..., off_width : off_width + width_len, off_long : off_long + long_len]
            )
            summed = weighted if summed is None else summed + weighted
    return summed


def combine_operator(negative, mass, damping):
    real_out = negative[:, 0] - WAVE_SCALE * (mass[:, 0] - damping * mass[:, 1])
    imag_out = negative[:, 1] - WAVE_SCALE * (mass[:, 1] + damping * mass[:, 0])
    return jnp.stack([real_out, imag_out], axis=1)


def inverse_diagonal(slowness, damping):
    scaled = WAVE_SCALE * MASS_WEIGHTS[1] * MASS_WEIGHTS[1] * slowness
    diag_re = LUMPED_DIAG - scaled * (1.0 + SHIFT_IMAG * damping)
    diag_im = -scaled * (damping + SHIFT_IMAG)
    norm_sq = diag_re * diag_re + diag_im * diag_im
    return (diag_re / norm_sq, -diag_im / norm_sq)


def complex_scale(inv_re, inv_im, values):
    real_part = values[:, 0]
    imag_part = values[:, 1]
    return jnp.stack(
        [inv_re * real_part - inv_im * imag_part, inv_re * imag_part + inv_im * real_part], axis=1
    )


def per_device(
    warm_field, slowness_sq, adjoint_field, observed, source_cell, receiver_cell, pml_width
):
    shot_count, _, layer_len, width_len, long_len = warm_field.shape
    depth_index = lax.axis_index("depth")
    tile_index = lax.axis_index("tile")
    depth_count = lax.axis_size("depth")
    tile_count = lax.axis_size("tile")
    full_depth = layer_len * depth_count
    full_width = width_len * tile_count
    depth_cells = depth_index * layer_len + jnp.arange(layer_len, dtype=jnp.int32)
    width_cells = tile_index * width_len + jnp.arange(width_len, dtype=jnp.int32)
    width_wide = (tile_index * width_len - 1 + jnp.arange(width_len + 2, dtype=jnp.int32)).astype(
        jnp.float32
    )
    damping_wide = damping_field(
        pml_width, depth_cells.astype(jnp.float32), width_wide, full_depth * 1.0, full_width * 1.0
    )[:, :, None]
    damping = damping_wide[:, 1:-1]
    slowness_wide = extended(slowness_sq, (("tile", 1),), 1)

    def apply_operator(values):
        padded = extended(values, (("depth", 2), ("tile", 3)), 1)
        negative = laplacian_from_padded(pad_long(padded), layer_len, width_len, long_len)
        mass = lateral_smooth(pad_long(padded[:, :, 1:-1] * slowness_wide), width_len, long_len)
        return combine_operator(negative, mass, damping)

    cell_index = (
        depth_cells[:, None, None] * full_width + width_cells[None, :, None]
    ) * long_len + jnp.arange(long_len, dtype=jnp.int32)[None, None, :]
    hits = cell_index[None] == source_cell[:, None, None, None]
    source_re = jnp.where(hits, SOURCE_AMPLITUDE, 0.0).astype(jnp.float32)
    forcing = jnp.stack([source_re, jnp.zeros_like(source_re)], axis=1)
    residual = forcing - apply_operator(warm_field)

    shots_here = shot_count // depth_count
    reach = -(-(full_depth - 1) // width_len)
    halo = reach * width_len
    window = width_len + 2 * halo

    def with_neighbour_rows(block):
        pieces = [shifted(block, "tile", step) for step in range(reach, 0, -1)]
        pieces.append(block)
        pieces += [shifted(block, "tile", -step) for step in range(1, reach + 1)]
        return jnp.concatenate(pieces, axis=-2)

    spread = jnp.broadcast_to(slowness_sq[None], (depth_count,) + slowness_sq.shape)
    slowness_all = lax.all_to_all(spread, "depth", 0, 1, tiled=True)[0]
    slowness_ext = with_neighbour_rows(slowness_all)
    rows_ext = tile_index * width_len - halo + jnp.arange(window, dtype=jnp.int32)
    damping_ext = damping_field(
        pml_width,
        jnp.arange(full_depth, dtype=jnp.float32),
        rows_ext.astype(jnp.float32),
        full_depth * 1.0,
        full_width * 1.0,
    )[:, :, None]
    inv_re, inv_im = inverse_diagonal(slowness_ext, damping_ext)
    row_valid = ((rows_ext >= 0) & (rows_ext < full_width))[:, None]

    def couple(plane_in):
        return plane_coupling(
            jnp.pad(plane_in, [(0, 0)] * (plane_in.ndim - 2) + [(1, 1), (1, 1)]),
            window,
            long_len,
        )

    residual_t = lax.all_to_all(residual, "depth", 0, 2, tiled=True)
    if reach == 2:
        near = residual_t[:, :, full_depth // 2 :]
        early = with_neighbour_rows(residual_t[:, :, : full_depth // 2])
        zero_rows = jnp.zeros(near.shape, near.dtype)
        late = jnp.concatenate(
            [zero_rows, shifted(near, "tile", 1), near, shifted(near, "tile", -1), zero_rows], axis=-2
        )
        residual_ext = jnp.concatenate([early, late], axis=2)
    else:
        residual_ext = with_neighbour_rows(residual_t)
    previous = jnp.zeros((shots_here, 2, window, long_len), jnp.float32)
    layers_out = []
    for layer_no in range(full_depth):
        source_term = residual_ext[:, :, layer_no] + couple(previous)
        previous = jnp.where(
            row_valid, complex_scale(inv_re[layer_no], inv_im[layer_no], source_term), 0.0
        )
        layers_out.append(previous)
    cut = min(halo // 2 + 1, full_depth)
    downward_ext = jnp.stack(layers_out, axis=2)
    if cut < full_depth:
        late = with_neighbour_rows(downward_ext[:, :, cut:, halo : halo + width_len])
        downward_ext = jnp.concatenate([downward_ext[:, :, :cut], late], axis=2)
    previous = jnp.zeros((shots_here, 2, window, long_len), jnp.float32)
    layers_out = [None] * full_depth
    for layer_no in range(full_depth - 1, -1, -1):
        previous = jnp.where(
            row_valid,
            downward_ext[:, :, layer_no]
            + complex_scale(inv_re[layer_no], inv_im[layer_no], couple(previous)),
            0.0,
        )
        layers_out[layer_no] = previous[:, :, halo : halo + width_len]
    search_t = jnp.stack(layers_out, axis=2)
    search = lax.all_to_all(search_t, "depth", 2, 0, tiled=True)
    image_field = apply_operator(search)
    local_real = jnp.sum(
        image_field[:, 0] * residual[:, 0] + image_field[:, 1] * residual[:, 1], axis=(1, 2, 3)
    )
    local_imag = jnp.sum(
        image_field[:, 0] * residual[:, 1] - image_field[:, 1] * residual[:, 0], axis=(1, 2, 3)
    )
    local_norm = jnp.sum(
        image_field[:, 0] * image_field[:, 0] + image_field[:, 1] * image_field[:, 1],
        axis=(1, 2, 3),
    )
    plane_cells = full_width * long_len
    rec_depth = receiver_cell // plane_cells
    rec_width = receiver_cell // long_len % full_width
    rec_long = receiver_cell % long_len
    local_depth = rec_depth - depth_index * layer_len
    local_width = rec_width - tile_index * width_len
    is_owned = (
        (local_depth >= 0)
        & (local_depth < layer_len)
        & (local_width >= 0)
        & (local_width < width_len)
    )
    row_count = layer_len * width_len
    local_row = jnp.where(is_owned, local_depth * width_len + local_width, -1)
    row_hot = (local_row[:, :, None] == jnp.arange(row_count, dtype=jnp.int32)).astype(jnp.float32)
    both_fields = jnp.concatenate([warm_field, search], axis=1).reshape(
        shot_count, 4, row_count, long_len
    )
    picked_rows = jnp.einsum(
        "srk,sqky->sqry", row_hot, both_fields, precision=lax.Precision.HIGHEST
    )
    col_hot = rec_long[:, None, :, None] == jnp.arange(long_len, dtype=jnp.int32)
    picked = jnp.sum(jnp.where(col_hot, picked_rows, 0.0), axis=-1)
    gap_re = picked[:, 0] - observed[:, 0]
    gap_im = picked[:, 1] - observed[:, 1]
    dir_re = picked[:, 2]
    dir_im = picked[:, 3]

    def owned_sum(values):
        return jnp.sum(jnp.where(is_owned, values, 0.0), axis=1)

    gap_norm = owned_sum(gap_re * gap_re + gap_im * gap_im)
    cross_re = owned_sum(gap_re * dir_re + gap_im * dir_im)
    cross_im = owned_sum(gap_re * dir_im - gap_im * dir_re)
    dir_norm = owned_sum(dir_re * dir_re + dir_im * dir_im)
    packed = jnp.stack(
        [local_real, local_imag, local_norm, gap_norm, cross_re, cross_im, dir_norm], axis=1
    )
    packed = all_sum(packed)
    dot_real, dot_imag, image_norm = packed[:, 0], packed[:, 1], packed[:, 2]
    gap_norm, cross_re, cross_im, dir_norm = packed[:, 3], packed[:, 4], packed[:, 5], packed[:, 6]
    step_re = (dot_real / image_norm)[:, None, None, None]
    step_im = (dot_imag / image_norm)[:, None, None, None]
    new_re = warm_field[:, 0] + step_re * search[:, 0] - step_im * search[:, 1]
    new_im = warm_field[:, 1] + step_re * search[:, 1] + step_im * search[:, 0]
    new_field = jnp.stack([new_re, new_im], axis=1)
    scale_re = dot_real / image_norm
    scale_im = dot_imag / image_norm
    misfit = 0.5 * (
        gap_norm
        + 2.0 * (scale_re * cross_re - scale_im * cross_im)
        + (scale_re * scale_re + scale_im * scale_im) * dir_norm
    )
    adjoint_wide = extended(adjoint_field, (("tile", 3),), 1)
    adjoint_re = adjoint_wide[:, 0]
    adjoint_im = adjoint_wide[:, 1]
    weight_re = adjoint_re + damping_wide * adjoint_im
    weight_im = damping_wide * adjoint_re - adjoint_im
    smooth_re = lateral_smooth(pad_long(weight_re), width_len, long_len)
    smooth_im = lateral_smooth(pad_long(weight_im), width_len, long_len)
    gradient = -WAVE_SCALE / shot_count * jnp.sum(new_re * smooth_re - new_im * smooth_im, axis=0)
    return (new_field, misfit, gradient)


def solution(mesh):
    return jax.shard_map(
        per_device,
        mesh=mesh,
        in_specs=(
            P(None, None, "depth", "tile", None),
            P("depth", "tile", None),
            P(None, None, "depth", "tile", None),
            P(),
            P(),
            P(),
            P(),
        ),
        out_specs=(P(None, None, "depth", "tile", None), P(), P("depth", "tile", None)),
        check_vma=False,
    )
```
